32 devices in a mesh: gx: 4 (over z), gy: 2 (over core), gz: 4 (over y, x).
Axes of the slice: x: 2, y: 2, z: 4, core: 2. Of those that a mesh axis runs over, the one named last changes fastest.
Arguments:
- e_field: float32 [3, 16, 32, 512], P(None, 'gx', 'gy', 'gz'), may hold values from -6 to 6
- h_field: float32 [3, 16, 32, 512], P(None, 'gx', 'gy', 'gz'), may hold values from -6 to 6
- current: float32 [3, 16, 32, 512], P(None, 'gx', 'gy', 'gz'), may hold values from -6 to 6
- material: int32 [16, 32, 512], P('gx', 'gy', 'gz'), may hold values from 0 to 2
- sigma_table: float32 [3], replicated, may hold values from 0.05 to 2
- gamma_table: float32 [3], replicated, may hold values from 0.05 to 1
- plasma_table: float32 [3], replicated, may hold values from 0.3 to 2
- g_kernel: float32 [4], replicated, may hold values from -4 to 4
- surf_cell: int32 [4, 2, 4, 1024], P('gx', 'gy', 'gz'), may hold values from 0 to 8191
- surf_owner: int32 [4, 2, 4, 1024, 1], P('gx', 'gy', 'gz'), may hold values from 0 to 7; in each aligned block of 1024 rows (0 to 1023, 1024 to 2047, ..., all dimensions but the last counted through in order) at most 192 rows name the same one
- surf_tile: int32 [4, 2, 4, 1024], P('gx', 'gy', 'gz'), may hold values from 0 to 127
- surf_normal: int32 [4, 2, 4, 1024], P('gx', 'gy', 'gz'), may hold values from 0 to 5
- row_count: int32 [4, 2, 4], P('gx', 'gy', 'gz'), may hold values from 256 to 1024, as said below
Outputs:
- e_out: float32 [3, 16, 32, 512], P(None, 'gx', 'gy', 'gz')
- h_out: float32 [3, 16, 32, 512], P(None, 'gx', 'gy', 'gz')
- force: float32 [3, 4096], P(None, ('gx', 'gy', 'gz'))
The draws below stay inside these ranges and needn't reach their ends.
Inputs may be any that keep to these rules, and one draw needn't show every extreme that they name: `surf_owner`: among the slots of one device no owner is named more than 192 times, a bound that some block reaches. `row_count`: some brick has all 1024 slots live.
All inputs are finite; a program needn't handle non-finite values.
Results may differ from the reference program's by a relative error of at most 0.00019.
Values sent between devices are 32-bit elements; how exact they have to be, the bound alone decides.
No kernel may reach another device: no remote copies, remote signals or barrier semaphores. Data moves between devices by JAX's collectives and lax.ppermute only.
A program may use at most 64 MiB of HBM per device.

```python
import math
import jax
import jax.numpy as jnp
import numpy as np
from jax import lax

CX = 4
CY = 16
CZ = 128
STEPS = 4
MATERIALS = 3
SLOTS = 1024
TILE_DEV = 128
CAP = 192
NX = 16
NY = 32
NZ = 512
TILES = 4096
N_GX = 4
N_GY = 2
N_GZ = 4


def draw_row_count(key, part):
    bricks = N_GX * N_GY * N_GZ
    key_a, key_b, key_c = jax.random.split(key, 3)
    row_loads = jax.random.randint(key_a, (bricks,), SLOTS // 4, SLOTS + 1, dtype=jnp.int32)
    first = jax.random.randint(key_b, (), 0, bricks, dtype=jnp.int32)
    second = (first + 1 + jax.random.randint(key_c, (), 0, bricks - 1, dtype=jnp.int32)) % bricks
    row_loads = row_loads.at[second].set(SLOTS // 4)
    row_loads = row_loads.at[first].set(SLOTS)
    return row_loads.reshape(N_GX, N_GY, N_GZ)


def with_ends(drawn, rng, low, high):
    index_at = [jax.random.randint(jax.random.fold_in(rng, axis), (), 0, length) for axis, length in enumerate(drawn.shape)]
    main_axis = drawn.shape.index(max(drawn.shape))
    beside = index_at[:main_axis] + [(index_at[main_axis] + 1) % drawn.shape[main_axis]] + index_at[main_axis + 1:]
    return drawn.at[tuple(index_at)].set(low).at[tuple(beside)].set(high)


def steps_of(rng, dims, pieces, low, largest):
    def one(position, blocks):
        heights = jax.random.uniform(jax.random.fold_in(jax.random.fold_in(rng, 6), position), (blocks,), jnp.float32, low / len(pieces), largest / len(pieces))
        return jnp.repeat(jnp.exp(heights), dims[position] // blocks).reshape((-1,) + (1,) * (len(dims) - position - 1))

    level = one(*pieces[0])
    for cut in pieces[1:]:
        level = level * one(*cut)
    return level


def routed_block(key, own, number, rows, amount, top, limit, slope):
    ranking = jax.random.permutation(key, amount)
    crowded, common = portions_of(amount, rows * top, limit, slope, True), portions_of(amount, rows * top, limit, slope, False)
    places = jnp.arange(amount)

    def named(tallies, offset_by):
        used = int((tallies > 0).sum())
        fixed = max(1, used // 4)
        shifted = fixed + (places - fixed + offset_by * (used - fixed)) % max(1, amount - fixed)
        return jnp.zeros((amount,), jnp.int32).at[ranking[jnp.where(places < fixed, places, shifted)]].set(jnp.asarray(tallies, jnp.int32))

    tallies = jnp.where(number % 4 == 0, named(crowded, number // 4), named(common, number - number // 4 - 1))
    mixed = jax.random.permutation(jax.random.fold_in(own, 3), amount)
    donor, sink = mixed[0:amount // 2 * 2:2], mixed[1:amount // 2 * 2:2]
    margin = jnp.minimum(tallies[donor] - 1, limit - tallies[sink]) // 2
    margin = jnp.where((donor == ranking[0]) | (sink == ranking[0]) | (tallies[sink] == 0), 0, jnp.maximum(margin, 0))
    shifted = jax.random.randint(jax.random.fold_in(own, 4), (amount // 2,), 0, 1 << 20) % (margin + 1)
    tallies = tallies.at[donor].add(-shifted).at[sink].add(shifted)
    items = jnp.searchsorted(jnp.cumsum(tallies), jnp.arange(rows * top), side="right").astype(jnp.int32)
    listing = items.reshape(top, rows).T
    listing = listing[jax.random.permutation(jax.random.fold_in(own, 1), rows)]
    offset_by = jax.random.randint(jax.random.fold_in(own, 2), (rows, 1), 0, top)
    return jnp.take_along_axis(listing, (jnp.arange(top)[None, :] + offset_by) % top, axis=1)


def portions_of(number_of, total, bound, slope, full):
    portions = [(1 << 20) // math.isqrt(rank ** slope) + 1 for rank in range(1, number_of + 1)]
    largest = bound if full else min(bound, max(-(-total // number_of), total * portions[0] // sum(portions)))
    least = 1 if total - largest >= number_of - 1 else 0
    given, spare = [largest] + [least] * (number_of - 1), total - largest - least * (number_of - 1)
    while spare > 0:
        free = [i for i in range(1, number_of) if given[i] < largest] or [i for i in range(1, number_of) if given[i] < bound]
        whole, left = sum([portions[i] for i in free]), spare
        for i in free:
            extra = min(bound - given[i], max(1, left * portions[i] // whole), spare)
            given[i] = given[i] + extra
            spare = spare - extra
    return np.array(given)


def centred(own_key, shape, scale, reach, pieces=(), kind=jnp.bfloat16):
    drawn = scale * jax.random.normal(own_key, shape, jnp.float32)
    if pieces:
        drawn = drawn * steps_of(own_key, shape, pieces, -0.22, 0.18)
    return jnp.clip(drawn, -reach, reach).astype(kind)


def setup_inputs(seed: int = 0) -> dict:
    keys = jax.random.split(jax.random.key(seed), 14)
    e_field = centred(keys[0], (3, NX, NY, NZ), 1.0, 6.0, ((1, 4), (2, 2), (3, 4)), jnp.float32)
    h_field = centred(keys[1], (3, NX, NY, NZ), 1.0, 6.0, ((1, 4), (2, 2), (3, 4)), jnp.float32)
    current = centred(keys[2], (3, NX, NY, NZ), 1.0, 6.0, ((1, 4), (2, 2), (3, 4)), jnp.float32)
    material = with_ends(jax.random.randint(keys[3], (NX, NY, NZ), 0, MATERIALS), jax.random.fold_in(keys[3], 1), 0, MATERIALS - 1).astype(jnp.int32)
    sigma_table = jnp.clip(jnp.exp(jax.random.uniform(keys[4], (MATERIALS,), jnp.float32, math.log(0.05), math.log(2.0))), 0.05, 2.0)
    gamma_table = jnp.clip(jnp.exp(jax.random.uniform(keys[5], (MATERIALS,), jnp.float32, math.log(0.05), math.log(1.0))), 0.05, 1.0)
    plasma_table = jnp.clip(jnp.exp(jax.random.uniform(keys[6], (MATERIALS,), jnp.float32, math.log(0.3), math.log(2.0))), 0.3, 2.0)
    g_kernel = centred(keys[7], (STEPS,), 1.0, 4.0, (), jnp.float32)
    surf_cell = with_ends(jax.random.randint(keys[8], (N_GX, N_GY, N_GZ, SLOTS), 0, CX * CY * CZ), jax.random.fold_in(keys[8], 1), 0, (CX * CY * CZ) - 1).astype(jnp.int32)
    surf_owner_keys = jax.random.split(jax.random.fold_in(keys[9], 1), N_GX * N_GY * N_GZ * SLOTS // SLOTS)
    surf_owner_turns = jax.random.permutation(jax.random.fold_in(keys[9], 3), N_GX * N_GY * N_GZ * SLOTS // SLOTS)
    surf_owner = jax.vmap(lambda own, number: routed_block(jax.random.fold_in(keys[9], 2), own, number, SLOTS, N_GX * N_GY, 1, CAP, 2))(surf_owner_keys, surf_owner_turns).reshape((N_GX, N_GY, N_GZ, SLOTS, 1))
    surf_tile = with_ends(jax.random.randint(keys[10], (N_GX, N_GY, N_GZ, SLOTS), 0, TILE_DEV), jax.random.fold_in(keys[10], 1), 0, TILE_DEV - 1).astype(jnp.int32)
    surf_normal = with_ends(jax.random.randint(keys[11], (N_GX, N_GY, N_GZ, SLOTS), 0, 6), jax.random.fold_in(keys[11], 1), 0, 5).astype(jnp.int32)
    row_count = draw_row_count(jax.random.fold_in(keys[13], 71), 0)
    return dict(e_field=e_field, h_field=h_field, current=current, material=material, sigma_table=sigma_table, gamma_table=gamma_table, plasma_table=plasma_table, g_kernel=g_kernel, surf_cell=surf_cell, surf_owner=surf_owner, surf_tile=surf_tile, surf_normal=surf_normal, row_count=row_count)


STEP_DT = 0.5
FACE_AREA = 0.25


def forward_curl(padded):
    elec_x, elec_y, elec_z = padded[0], padded[1], padded[2]
    curl_x = (elec_z[:-1, 1:, :-1] - elec_z[:-1, :-1, :-1]) - (elec_y[:-1, :-1, 1:] - elec_y[:-1, :-1, :-1])
    curl_y = (elec_x[:-1, :-1, 1:] - elec_x[:-1, :-1, :-1]) - (elec_z[1:, :-1, :-1] - elec_z[:-1, :-1, :-1])
    curl_z = (elec_y[1:, :-1, :-1] - elec_y[:-1, :-1, :-1]) - (elec_x[:-1, 1:, :-1] - elec_x[:-1, :-1, :-1])
    return jnp.stack([curl_x, curl_y, curl_z])


def backward_curl(padded):
    magn_x, magn_y, magn_z = padded[0], padded[1], padded[2]
    curl_x = (magn_z[1:, 1:, 1:] - magn_z[1:, :-1, 1:]) - (magn_y[1:, 1:, 1:] - magn_y[1:, 1:, :-1])
    curl_y = (magn_x[1:, 1:, 1:] - magn_x[1:, 1:, :-1]) - (magn_z[1:, 1:, 1:] - magn_z[:-1, 1:, 1:])
    curl_z = (magn_y[1:, 1:, 1:] - magn_y[:-1, 1:, 1:]) - (magn_x[1:, 1:, 1:] - magn_x[1:, :-1, 1:])
    return jnp.stack([curl_x, curl_y, curl_z])


def lookup(material, table):
    result = jnp.zeros(material.shape, table.dtype)
    for which in range(table.shape[0]):
        result = result + jnp.where(material == which, table[which], jnp.zeros((), table.dtype))
    return result


def coefficients(material, sigma_table, gamma_table, plasma_table):
    sigma = lookup(material, sigma_table)
    gamma = lookup(material, gamma_table)
    plasma = lookup(material, plasma_table)
    keep_e = (1.0 - sigma * STEP_DT / 2) / (1.0 + sigma * STEP_DT / 2)
    gain_e = STEP_DT / (1.0 + sigma * STEP_DT / 2)
    keep_j = (1.0 - gamma * STEP_DT / 2) / (1.0 + gamma * STEP_DT / 2)
    gain_j = plasma * STEP_DT / (1.0 + gamma * STEP_DT / 2)
    return keep_e, gain_e, keep_j, gain_j


def row_forces(elec_rows, magn_rows, normal):
    axis_of = normal // 2
    sign_of = (1 - 2 * (normal % 2)).astype(elec_rows.dtype)
    picked = (axis_of[None, :] == jnp.arange(3, dtype=jnp.int32)[:, None]).astype(elec_rows.dtype)
    elec_n = jnp.sum(elec_rows * picked, axis=0)
    magn_n = jnp.sum(magn_rows * picked, axis=0)
    energy = 0.5 * (jnp.sum(elec_rows * elec_rows, axis=0) + jnp.sum(magn_rows * magn_rows, axis=0))
    return sign_of * (elec_rows * elec_n + magn_rows * magn_n - picked * energy)


def reference(e_field, h_field, current, material, sigma_table, gamma_table, plasma_table, g_kernel, surf_cell, surf_owner, surf_tile, surf_normal, row_count):
    keep_e, gain_e, keep_j, gain_j = coefficients(material, sigma_table, gamma_table, plasma_table)
    electric, magnetic, drude = e_field, h_field, current
    grid_shape = (N_GX, N_GY, N_GZ, SLOTS)
    brick_x = lax.broadcasted_iota(jnp.int32, grid_shape, 0)
    brick_y = lax.broadcasted_iota(jnp.int32, grid_shape, 1)
    brick_z = lax.broadcasted_iota(jnp.int32, grid_shape, 2)
    slot_pos = lax.broadcasted_iota(jnp.int32, grid_shape, 3)
    glob_x = (brick_x * CX + surf_cell // (CY * CZ)).reshape(-1)
    glob_y = (brick_y * CY + (surf_cell // CZ) % CY).reshape(-1)
    glob_z = (brick_z * CZ + surf_cell % CZ).reshape(-1)
    normal = surf_normal.reshape(-1)
    live_mask = (slot_pos < row_count[:, :, :, None]).astype(e_field.dtype).reshape(-1)
    summed = jnp.zeros((3, normal.shape[0]), e_field.dtype)
    for moment in range(STEPS):
        magnetic = magnetic - STEP_DT * forward_curl(jnp.pad(electric, ((0, 0), (0, 1), (0, 1), (0, 1))))
        drude = keep_j * drude + gain_j * electric
        electric = keep_e * electric + gain_e * (backward_curl(jnp.pad(magnetic, ((0, 0), (1, 0), (1, 0), (1, 0)))) - drude)
        elec_rows = electric[:, glob_x, glob_y, glob_z]
        magn_rows = magnetic[:, glob_x, glob_y, glob_z]
        summed = summed + g_kernel[moment] * row_forces(elec_rows, magn_rows, normal)
    row_force = FACE_AREA * summed * live_mask
    segment = ((surf_owner.reshape(-1) * N_GZ + brick_z.reshape(-1)) * TILE_DEV + surf_tile.reshape(-1)).astype(jnp.int32)
    force = jax.ops.segment_sum(row_force.T, segment, num_segments=TILES).T
    return electric, magnetic, force
```

```python
import functools

import jax
import jax.numpy as jnp
from jax import lax
from jax.experimental import pallas as pl
from jax.experimental.pallas import tpu as pltpu
from jax.sharding import PartitionSpec as P

STEP_DT = 0.5
FACE_AREA = 0.25
TILE_DEV = 128
PAIRS = ((0, 0), (0, 1), (0, 2), (1, 1), (1, 2), (2, 2))
AXES = ("gx", "gy", "gz")
VMEM = pl.BlockSpec(memory_space=pltpu.VMEM)
SMEM = pl.BlockSpec(memory_space=pltpu.SMEM)


def partner(index, size, second):
    if not second:
        return index ^ 1
    return (index - 1) % size if index % 2 == 0 else (index + 1) % size


def full_swap(sizes, second_x=None, second_y=None, second_z=None, local_ends=False):
    n_x, n_y, n_z = sizes
    pairs = []
    for x in range(n_x):
        for y in range(n_y):
            for z in range(n_z):
                to = [x, y, z]
                if second_x is not None:
                    if local_ends and second_x and x in (0, n_x - 1):
                        to[1] = y ^ 1
                    else:
                        to[0] = partner(x, n_x, second_x)
                if second_y is not None:
                    to[1] = partner(y, n_y, second_y)
                if second_z is not None:
                    to[2] = partner(z, n_z, second_z)
                pairs.append(((x * n_y + y) * n_z + z, (to[0] * n_y + to[1]) * n_z + to[2]))
    return pairs


def fields_of(e_ref, h_ref, j_ref, m_ref, planes):
    out = []
    for ref in (e_ref, h_ref, j_ref):
        for comp in range(3):
            for plane in range(planes):
                out.append(ref[comp, plane])
    for plane in range(planes):
        out.append((m_ref[plane] + 1).astype(jnp.float32))
    return out


def pack_kernel(depth, e_ref, h_ref, j_ref, m_ref, brick_ref, even_ref, odd_ref):
    planes, rows, lanes = m_ref.shape
    per_tile = lanes // depth
    lane = lax.broadcasted_iota(jnp.int32, (rows, lanes), 1)
    group = lane // depth
    fields = fields_of(e_ref, h_ref, j_ref, m_ref, planes)
    tiles = even_ref.shape[0]
    low = [jnp.zeros((rows, lanes), jnp.float32) for _ in range(tiles)]
    high = [jnp.zeros((rows, lanes), jnp.float32) for _ in range(tiles)]
    for j, value in enumerate(fields):
        brick_ref[j] = value
        tile, slot = j // per_tile, j % per_tile
        up = pltpu.roll(value, depth * slot, 1) if slot else value
        down = pltpu.roll(value, lanes - depth * slot, 1) if slot else value
        low[tile] = jnp.where(group == slot, up, low[tile])
        high[tile] = jnp.where(group == per_tile - 1 - slot, down, high[tile])
    is_even = lax.axis_index("gz") % 2 == 0
    for tile in range(tiles):
        even_ref[tile] = jnp.where(is_even, high[tile], low[tile])
        odd_ref[tile] = jnp.where(is_even, low[tile], high[tile])


def rows_kernel(n_in, n_y, *refs):
    ins, outs = refs[:n_in], refs[n_in:]
    is_odd = lax.axis_index("gy") % 2
    at = 0
    for ref in ins:
        count, rows, _ = ref.shape
        for which, out in enumerate(outs):
            last = (1 - is_odd) if which == 0 else is_odd
            start = pl.multiple_of(last * (rows - 8), 8)
            out[pl.ds(at, count)] = ref[:, pl.ds(start, 8), :]
        at += count


def main_kernel(sizes, steps, materials, counts, *refs):
    n_x, n_y, n_z = sizes
    n_in = len(counts)
    n_ghost = 1 if n_y == 2 else 2
    parts, refs = refs[:n_in], refs[n_in:]
    ghosts, refs = refs[:n_ghost], refs[n_ghost:]
    sigma_ref, gamma_ref, plasma_ref, g_ref, count_ref = refs[:5]
    cell_ref, owner_ref, tile_ref, normal_ref = refs[5:9]
    e_out, h_out, part_out = refs[9:12]
    field, coef, gain_h, tensor = refs[12:16]
    _, rows, lanes = parts[0].shape
    planes = e_out.shape[1]
    depth = steps
    per_tile = lanes // depth
    x, y, z = (lax.axis_index(a) for a in AXES)
    even_x, even_y, even_z = x % 2 == 0, y % 2 == 0, z % 2 == 0
    low_x, high_x = x > 0, x < n_x - 1
    low_y, high_y = y > 0, y < n_y - 1
    low_z, high_z = z > 0, z < n_z - 1
    row8 = lax.broadcasted_iota(jnp.int32, (8, lanes), 0)
    lower_from = jnp.where(low_y, 8 - depth, 8)
    upper_to = jnp.where(high_y, depth, 0)
    lower_rows = row8 >= lower_from
    upper_rows = row8 < upper_to
    one_side = (row8 >= jnp.where(even_y, 0, lower_from)) & (row8 < jnp.where(even_y, upper_to, 8))

    offsets = [sum(counts[:i]) for i in range(n_in)]

    def ghost_rows(at):
        if n_ghost == 1:
            value = ghosts[0][at]
            return jnp.where(one_side, value, 0.0)
        first, second = ghosts[0][at], ghosts[1][at]
        upper = jnp.where(even_y, first, second)
        lower = jnp.where(even_y, second, first)
        return jnp.where(upper_rows, upper, jnp.where(lower_rows, lower, 0.0))

    def whole(part, j):
        return jnp.concatenate([parts[part][j], ghost_rows(offsets[part] + j)], 0)

    full_rows = rows + 8
    lane = lax.broadcasted_iota(jnp.int32, (full_rows, lanes), 1)
    upper_lanes = lane < jnp.where(high_z, depth, 0)
    lower_lanes = lane >= jnp.where(low_z, lanes - depth, lanes)
    n_fields = 10
    z_tiles = counts[3]

    def edges(base):
        out = []
        for tile in range(z_tiles):
            first, second = whole(base, tile), whole(base + 1, tile)
            out.append((jnp.where(even_z, first, second), jnp.where(even_z, second, first)))
        return out

    own_edges, first_edges, second_edges = edges(3), edges(5), edges(7)
    for cls in range(3):
        for j in range(n_fields * planes):
            tile, slot = j // per_tile, j % per_tile
            if cls == 1:
                main = whole(0, j)
                upper, lower = own_edges[tile]
            else:
                first, second = whole(1, j), whole(2, j)
                take_first = even_x if cls == 2 else jnp.logical_not(even_x)
                valid = high_x if cls == 2 else low_x
                main = jnp.where(valid, jnp.where(take_first, first, second), 0.0)
                upper = jnp.where(valid, jnp.where(take_first, first_edges[tile][0], second_edges[tile][0]), 0.0)
                lower = jnp.where(valid, jnp.where(take_first, first_edges[tile][1], second_edges[tile][1]), 0.0)
            if slot:
                upper = pltpu.roll(upper, lanes - depth * slot, 1)
                lower = pltpu.roll(lower, depth * slot, 1)
            side = jnp.where(upper_lanes, upper, jnp.where(lower_lanes, lower, 0.0))
            at = cls * planes + j % planes
            field[j // planes, at, :, :lanes] = main
            field[j // planes, at, :, lanes:] = side

    wide = 2 * lanes

    def splat(value):
        return jnp.full((8, lanes), value, jnp.float32)

    table = []
    for which in range(materials):
        sigma, gamma, plasma = splat(sigma_ref[which]), splat(gamma_ref[which]), splat(plasma_ref[which])
        table.append((
            (1.0 - sigma * STEP_DT / 2) / (1.0 + sigma * STEP_DT / 2),
            STEP_DT / (1.0 + sigma * STEP_DT / 2),
            (1.0 - gamma * STEP_DT / 2) / (1.0 + gamma * STEP_DT / 2),
            plasma * STEP_DT / (1.0 + gamma * STEP_DT / 2),
        ))
    for plane in range(1, 3 * planes - 1):
        for r in range(0, full_rows, 8):
            for c in range(0, wide, lanes):
                code = field[9, plane, r : r + 8, c : c + lanes]
                for which in range(4):
                    value = jnp.zeros((8, lanes), jnp.float32)
                    for m in range(materials):
                        value = jnp.where(code == float(m + 1), table[m][which], value)
                    coef[which, plane, r : r + 8, c : c + lanes] = value

    row = lax.broadcasted_iota(jnp.int32, (full_rows, wide), 0)
    col = lax.broadcasted_iota(jnp.int32, (full_rows, wide), 1)
    inside = (row < jnp.where(low_y, full_rows, full_rows - depth)) & (col < jnp.where(low_z, wide, wide - depth))
    gain = jnp.where(inside, STEP_DT, 0.0)
    gain_h[1] = gain
    gain_h[0] = jnp.where(low_x, gain, 0.0)

    def next_y(v):
        return pltpu.roll(v, full_rows - 1, 0)

    def next_z(v):
        return pltpu.roll(v, wide - 1, 1)

    def prev_y(v):
        return pltpu.roll(v, 1, 0)

    def prev_z(v):
        return pltpu.roll(v, 1, 1)

    last = 3 * planes - 1
    for t in range(1, steps + 1):
        for plane in range(t - 1, last - t + 1):
            ex, ey, ez = field[0, plane], field[1, plane], field[2, plane]
            hx, hy, hz = field[3, plane], field[4, plane], field[5, plane]
            ey_x, ez_x = field[1, plane + 1], field[2, plane + 1]
            dt = gain_h[0 if plane < planes else 1]
            hy = hy - dt * ((next_z(ex) - ex) - (ez_x - ez))
            hz = hz - dt * ((ey_x - ey) - (next_y(ex) - ex))
            field[4, plane] = hy
            field[5, plane] = hz
            if plane < t:
                continue
            hx = hx - dt * ((next_y(ez) - ez) - (next_z(ey) - ey))
            field[3, plane] = hx
            hy_x, hz_x = field[4, plane - 1], field[5, plane - 1]
            keep_e, gain_e, keep_j, gain_j = (coef[i, plane] for i in range(4))
            curl_x = (hz - prev_y(hz)) - (hy - prev_z(hy))
            curl_y = (hx - prev_z(hx)) - (hz - hz_x)
            curl_z = (hy - hy_x) - (hx - prev_y(hx))
            for comp, (old, curl) in enumerate(((ex, curl_x), (ey, curl_y), (ez, curl_z))):
                drude = keep_j * field[6 + comp, plane] + gain_j * old
                field[6 + comp, plane] = drude
                field[comp, plane] = keep_e * old + gain_e * (curl - drude)
        g = g_ref[t - 1]
        for plane in range(planes):
            e = [field[i, planes + plane, :rows, :lanes] for i in range(3)]
            h = [field[3 + i, planes + plane, :rows, :lanes] for i in range(3)]
            prod = {p: e[p[0]] * e[p[1]] + h[p[0]] * h[p[1]] for p in PAIRS}
            energy = 0.5 * (prod[0, 0] + prod[1, 1] + prod[2, 2])
            for i, p in enumerate(PAIRS):
                value = prod[p] - energy if p[0] == p[1] else prod[p]
                value = g * value
                if t > 1:
                    value = tensor[i, pl.ds(plane * rows, rows), :] + value
                tensor[i, pl.ds(plane * rows, rows), :] = value
            if t == steps:
                for i in range(3):
                    e_out[i, plane] = e[i]
                    h_out[i, plane] = h[i]

    def halves(v):
        high = v.astype(jnp.bfloat16)
        return high, (v - high.astype(jnp.float32)).astype(jnp.bfloat16)

    cells = planes * rows
    high, low = halves(tensor[...].reshape(len(PAIRS) * cells, lanes))
    lhs = jnp.concatenate([high, low], 1)
    slots = cell_ref.shape[1]
    owners = part_out.shape[0]
    chunk = 256
    total = jnp.zeros((2 * owners * 8, TILE_DEV), jnp.float32)
    for at in range(0, slots, chunk):
        cell = cell_ref[:, at : at + chunk]
        owner = owner_ref[:, at : at + chunk]
        normal = normal_ref[:, at : at + chunk]
        tile = tile_ref[:, at : at + chunk]
        live = (at + lax.broadcasted_iota(jnp.int32, (1, chunk), 1)) < count_ref[0]
        hot = jnp.where(lax.broadcasted_iota(jnp.int32, (lanes, chunk), 0) == cell % lanes, 1.0, 0.0).astype(jnp.bfloat16)
        picked = jnp.dot(lhs, jnp.concatenate([hot, hot], 0), preferred_element_type=jnp.float32)
        in_row = lax.broadcasted_iota(jnp.int32, (cells, chunk), 0) == cell // lanes
        vals = {
            p: jnp.sum(jnp.where(in_row, picked[i * cells : (i + 1) * cells], 0.0), axis=0, keepdims=True)
            for i, p in enumerate(PAIRS)
        }
        axis = normal // 2
        sign = (1 - 2 * (normal % 2)).astype(jnp.float32)
        scale = jnp.where(live, FACE_AREA * sign, 0.0)
        row_force = []
        for i in range(3):
            by = [vals[min(i, a), max(i, a)] for a in range(3)]
            row_force.append(scale * jnp.where(axis == 0, by[0], jnp.where(axis == 1, by[1], by[2])))
        stacked = jnp.concatenate(row_force + [jnp.zeros((5, chunk), jnp.float32)], 0)
        spread = jnp.concatenate([jnp.where(owner == o, stacked, 0.0) for o in range(owners)], 0)
        a_high, a_low = halves(spread)
        a = jnp.concatenate([a_high, a_low], 0)
        tile_hot = jnp.where(lax.broadcasted_iota(jnp.int32, (TILE_DEV, chunk), 0) == tile, 1.0, 0.0).astype(jnp.bfloat16)
        total = total + lax.dot_general(a, tile_hot, (((1,), (1,)), ((), ())), preferred_element_type=jnp.float32)
    part = total[: owners * 8] + total[owners * 8 :]
    for o in range(owners):
        part_out[o] = part[o * 8 : (o + 1) * 8]


def local(sizes, e_field, h_field, current, material, sigma_table, gamma_table, plasma_table, g_kernel,
          surf_cell, surf_owner, surf_tile, surf_normal, row_count):
    n_x, n_y, n_z = sizes
    steps = g_kernel.shape[0]
    planes, rows, lanes = material.shape
    f32 = jnp.float32
    n_msg = 10 * planes
    z_tiles = -(-n_msg * steps // lanes)
    brick, z_first, z_second = pl.pallas_call(
        functools.partial(pack_kernel, steps),
        out_shape=(
            jax.ShapeDtypeStruct((n_msg, rows, lanes), f32),
            jax.ShapeDtypeStruct((z_tiles, rows, lanes), f32),
            jax.ShapeDtypeStruct((z_tiles, rows, lanes), f32),
        ),
        in_specs=[VMEM] * 4,
        out_specs=(VMEM,) * 3,
        name="pack",
    )(e_field, h_field, current, material)

    def send(value, **how):
        return lax.ppermute(value, AXES, full_swap(sizes, **how))

    parts = [
        brick,
        send(brick, second_x=False),
        send(brick, second_x=True, local_ends=True),
        send(z_first, second_z=False),
        send(z_second, second_z=True),
        send(z_first, second_x=False, second_z=False),
        send(z_second, second_x=False, second_z=True),
        send(z_first, second_x=True, second_z=False),
        send(z_second, second_x=True, second_z=True),
    ]
    counts = [p.shape[0] for p in parts]
    n_ghost = 1 if n_y == 2 else 2
    outgoing = pl.pallas_call(
        functools.partial(rows_kernel, len(parts), n_y),
        out_shape=[jax.ShapeDtypeStruct((sum(counts), 8, lanes), f32)] * n_ghost,
        in_specs=[VMEM] * len(parts),
        out_specs=[VMEM] * n_ghost,
        name="rows",
    )(*parts)
    ghosts = [send(v, second_y=bool(i)) for i, v in enumerate(outgoing)]

    owners = n_x * n_y
    slots = surf_cell.size
    wide = 2 * lanes
    e_out, h_out, part = pl.pallas_call(
        functools.partial(main_kernel, sizes, steps, sigma_table.shape[0], counts),
        out_shape=(
            jax.ShapeDtypeStruct(e_field.shape, f32),
            jax.ShapeDtypeStruct(h_field.shape, f32),
            jax.ShapeDtypeStruct((owners, 8, TILE_DEV), f32),
        ),
        in_specs=[VMEM] * (len(parts) + n_ghost) + [SMEM] * 5 + [VMEM] * 4,
        out_specs=(VMEM,) * 3,
        scratch_shapes=[
            pltpu.VMEM((10, 3 * planes, rows + 8, wide), f32),
            pltpu.VMEM((4, 3 * planes, rows + 8, wide), f32),
            pltpu.VMEM((2, rows + 8, wide), f32),
            pltpu.VMEM((len(PAIRS), planes * rows, lanes), f32),
        ],
        name="march",
    )(*parts, *ghosts, sigma_table, gamma_table, plasma_table, g_kernel, row_count.reshape(1),
      surf_cell.reshape(1, slots), surf_owner.reshape(1, slots), surf_tile.reshape(1, slots), surf_normal.reshape(1, slots))
    got = lax.all_to_all(part, ("gx", "gy"), split_axis=0, concat_axis=0, tiled=True)
    force = jnp.sum(got, axis=0)[:3]
    return e_out, h_out, force


def solution(mesh):
    sizes = tuple(mesh.shape[a] for a in AXES)
    return jax.shard_map(
        functools.partial(local, sizes),
        mesh=mesh,
        in_specs=(
            P(None, "gx", "gy", "gz"),
            P(None, "gx", "gy", "gz"),
            P(None, "gx", "gy", "gz"),
            P("gx", "gy", "gz"),
            P(),
            P(),
            P(),
            P(),
            P("gx", "gy", "gz", None),
            P("gx", "gy", "gz", None, None),
            P("gx", "gy", "gz", None),
            P("gx", "gy", "gz", None),
            P("gx", "gy", "gz"),
        ),
        out_specs=(
            P(None, "gx", "gy", "gz"),
            P(None, "gx", "gy", "gz"),
            P(None, ("gx", "gy", "gz")),
        ),
        check_vma=False,
    )
```

```python
import functools

import jax
import jax.numpy as jnp
from jax import lax
from jax.experimental import pallas as pl
from jax.experimental.pallas import tpu as pltpu
from jax.sharding import PartitionSpec as P

STEP_DT = 0.5
FACE_AREA = 0.25
TILE_DEV = 128
PAIRS = ((0, 0), (0, 1), (0, 2), (1, 1), (1, 2), (2, 2))
AXES = ("gx", "gy", "gz")
VMEM = pl.BlockSpec(memory_space=pltpu.VMEM)
SMEM = pl.BlockSpec(memory_space=pltpu.SMEM)


def partner(index, size, second):
    if not second:
        return index ^ 1
    return (index - 1) % size if index % 2 == 0 else (index + 1) % size


def full_swap(sizes, axis, second=False):
    pairs = []
    at = AXES.index(axis)
    for x in range(sizes[0]):
        for y in range(sizes[1]):
            for z in range(sizes[2]):
                to = [x, y, z]
                if second and to[at] in (0, sizes[at] - 1) and axis != "gy":
                    to[1] = y ^ 1
                else:
                    to[at] = partner(to[at], sizes[at], second)
                pairs.append(((x * sizes[1] + y) * sizes[2] + z, (to[0] * sizes[1] + to[1]) * sizes[2] + to[2]))
    return pairs


def fields_of(e_ref, h_ref, j_ref, m_ref, planes):
    out = []
    for ref in (e_ref, h_ref, j_ref):
        for comp in range(3):
            for plane in range(planes):
                out.append(ref[comp, plane])
    for plane in range(planes):
        out.append((m_ref[plane] + 1).astype(jnp.float32))
    return out


def pack_kernel(depth, e_ref, h_ref, j_ref, m_ref, brick_ref, even_ref, odd_ref):
    planes, rows, lanes = m_ref.shape
    per_tile = lanes // depth
    lane = lax.broadcasted_iota(jnp.int32, (rows, lanes), 1)
    group = lane // depth
    fields = fields_of(e_ref, h_ref, j_ref, m_ref, planes)
    tiles = even_ref.shape[0]
    low = [jnp.zeros((rows, lanes), jnp.float32) for _ in range(tiles)]
    high = [jnp.zeros((rows, lanes), jnp.float32) for _ in range(tiles)]
    for j, value in enumerate(fields):
        brick_ref[j] = value
        tile, slot = j // per_tile, j % per_tile
        up = pltpu.roll(value, depth * slot, 1) if slot else value
        down = pltpu.roll(value, lanes - depth * slot, 1) if slot else value
        low[tile] = jnp.where(group == slot, up, low[tile])
        high[tile] = jnp.where(group == per_tile - 1 - slot, down, high[tile])
    is_even = lax.axis_index("gz") % 2 == 0
    for tile in range(tiles):
        even_ref[tile] = jnp.where(is_even, high[tile], low[tile])
        odd_ref[tile] = jnp.where(is_even, low[tile], high[tile])


def rows_kernel(n_in, n_y, *refs):
    ins, outs = refs[:n_in], refs[n_in:]
    is_odd = lax.axis_index("gy") % 2
    at = 0
    for ref in ins:
        count, rows, _ = ref.shape
        for which, out in enumerate(outs):
            last = (1 - is_odd) if which == 0 else is_odd
            start = pl.multiple_of(last * (rows - 8), 8)
            out[pl.ds(at, count)] = ref[:, pl.ds(start, 8), :]
        at += count


def main_kernel(sizes, steps, materials, counts, *refs):
    n_x, n_y, n_z = sizes
    n_in = len(counts)
    n_ghost = 1 if n_y == 2 else 2
    parts, refs = refs[:n_in], refs[n_in:]
    ghosts, refs = refs[:n_ghost], refs[n_ghost:]
    sigma_ref, gamma_ref, plasma_ref, g_ref, count_ref = refs[:5]
    cell_ref, owner_ref, tile_ref, normal_ref = refs[5:9]
    e_out, h_out, part_out = refs[9:12]
    field, coef, gain_h, tensor = refs[12:16]
    _, rows, lanes = parts[0].shape
    planes = e_out.shape[1]
    depth = steps
    per_tile = lanes // depth
    x, y, z = (lax.axis_index(a) for a in AXES)
    even_x, even_y, even_z = x % 2 == 0, y % 2 == 0, z % 2 == 0
    low_x, high_x = x > 0, x < n_x - 1
    low_y, high_y = y > 0, y < n_y - 1
    low_z, high_z = z > 0, z < n_z - 1
    row8 = lax.broadcasted_iota(jnp.int32, (8, lanes), 0)
    lower_from = jnp.where(low_y, 8 - depth, 8)
    upper_to = jnp.where(high_y, depth, 0)
    lower_rows = row8 >= lower_from
    upper_rows = row8 < upper_to
    one_side = (row8 >= jnp.where(even_y, 0, lower_from)) & (row8 < jnp.where(even_y, upper_to, 8))

    offsets = [sum(counts[:i]) for i in range(n_in)]

    def ghost_rows(at):
        if n_ghost == 1:
            value = ghosts[0][at]
            return jnp.where(one_side, value, 0.0)
        first, second = ghosts[0][at], ghosts[1][at]
        upper = jnp.where(even_y, first, second)
        lower = jnp.where(even_y, second, first)
        return jnp.where(upper_rows, upper, jnp.where(lower_rows, lower, 0.0))

    def whole(part, j):
        return jnp.concatenate([parts[part][j], ghost_rows(offsets[part] + j)], 0)

    full_rows = rows + 8
    lane = lax.broadcasted_iota(jnp.int32, (full_rows, lanes), 1)
    upper_lanes = lane < jnp.where(high_z, depth, 0)
    lower_lanes = lane >= jnp.where(low_z, lanes - depth, lanes)
    n_fields = 10
    z_tiles = counts[3]

    def edges(base):
        out = []
        for tile in range(z_tiles):
            first, second = whole(base, tile), whole(base + 1, tile)
            out.append((jnp.where(even_z, first, second), jnp.where(even_z, second, first)))
        return out

    own_edges, first_edges, second_edges = edges(3), edges(5), edges(7)
    for cls in range(3):
        for j in range(n_fields * planes):
            tile, slot = j // per_tile, j % per_tile
            if cls == 1:
                main = whole(0, j)
                upper, lower = own_edges[tile]
            else:
                first, second = whole(1, j), whole(2, j)
                take_first = even_x if cls == 2 else jnp.logical_not(even_x)
                valid = high_x if cls == 2 else low_x
                main = jnp.where(valid, jnp.where(take_first, first, second), 0.0)
                upper = jnp.where(valid, jnp.where(take_first, first_edges[tile][0], second_edges[tile][0]), 0.0)
                lower = jnp.where(valid, jnp.where(take_first, first_edges[tile][1], second_edges[tile][1]), 0.0)
            if slot:
                upper = pltpu.roll(upper, lanes - depth * slot, 1)
                lower = pltpu.roll(lower, depth * slot, 1)
            side = jnp.where(upper_lanes, upper, jnp.where(lower_lanes, lower, 0.0))
            at = cls * planes + j % planes
            field[j // planes, at, :, :lanes] = main
            field[j // planes, at, :, lanes:] = side

    wide = 2 * lanes

    def splat(value):
        return jnp.full((8, lanes), value, jnp.float32)

    table = []
    for which in range(materials):
        sigma, gamma, plasma = splat(sigma_ref[which]), splat(gamma_ref[which]), splat(plasma_ref[which])
        table.append((
            (1.0 - sigma * STEP_DT / 2) / (1.0 + sigma * STEP_DT / 2),
            STEP_DT / (1.0 + sigma * STEP_DT / 2),
            (1.0 - gamma * STEP_DT / 2) / (1.0 + gamma * STEP_DT / 2),
            plasma * STEP_DT / (1.0 + gamma * STEP_DT / 2),
        ))
    for plane in range(1, 3 * planes - 1):
        for r in range(0, full_rows, 8):
            for c in range(0, wide, lanes):
                code = field[9, plane, r : r + 8, c : c + lanes]
                for which in range(4):
                    value = jnp.zeros((8, lanes), jnp.float32)
                    for m in range(materials):
                        value = jnp.where(code == float(m + 1), table[m][which], value)
                    coef[which, plane, r : r + 8, c : c + lanes] = value

    row = lax.broadcasted_iota(jnp.int32, (full_rows, wide), 0)
    col = lax.broadcasted_iota(jnp.int32, (full_rows, wide), 1)
    inside = (row < jnp.where(low_y, full_rows, full_rows - depth)) & (col < jnp.where(low_z, wide, wide - depth))
    gain = jnp.where(inside, STEP_DT, 0.0)
    gain_h[1] = gain
    gain_h[0] = jnp.where(low_x, gain, 0.0)

    def next_y(v):
        return pltpu.roll(v, full_rows - 1, 0)

    def next_z(v):
        return pltpu.roll(v, wide - 1, 1)

    def prev_y(v):
        return pltpu.roll(v, 1, 0)

    def prev_z(v):
        return pltpu.roll(v, 1, 1)

    last = 3 * planes - 1
    for t in range(1, steps + 1):
        for plane in range(t - 1, last - t + 1):
            ex, ey, ez = field[0, plane], field[1, plane], field[2, plane]
            hx, hy, hz = field[3, plane], field[4, plane], field[5, plane]
            ey_x, ez_x = field[1, plane + 1], field[2, plane + 1]
            dt = gain_h[0 if plane < planes else 1]
            hy = hy - dt * ((next_z(ex) - ex) - (ez_x - ez))
            hz = hz - dt * ((ey_x - ey) - (next_y(ex) - ex))
            field[4, plane] = hy
            field[5, plane] = hz
            if plane < t:
                continue
            hx = hx - dt * ((next_y(ez) - ez) - (next_z(ey) - ey))
            field[3, plane] = hx
            hy_x, hz_x = field[4, plane - 1], field[5, plane - 1]
            keep_e, gain_e, keep_j, gain_j = (coef[i, plane] for i in range(4))
            curl_x = (hz - prev_y(hz)) - (hy - prev_z(hy))
            curl_y = (hx - prev_z(hx)) - (hz - hz_x)
            curl_z = (hy - hy_x) - (hx - prev_y(hx))
            for comp, (old, curl) in enumerate(((ex, curl_x), (ey, curl_y), (ez, curl_z))):
                drude = keep_j * field[6 + comp, plane] + gain_j * old
                field[6 + comp, plane] = drude
                field[comp, plane] = keep_e * old + gain_e * (curl - drude)
        g = g_ref[t - 1]
        for plane in range(planes):
            e = [field[i, planes + plane, :rows, :lanes] for i in range(3)]
            h = [field[3 + i, planes + plane, :rows, :lanes] for i in range(3)]
            prod = {p: e[p[0]] * e[p[1]] + h[p[0]] * h[p[1]] for p in PAIRS}
            energy = 0.5 * (prod[0, 0] + prod[1, 1] + prod[2, 2])
            for i, p in enumerate(PAIRS):
                value = prod[p] - energy if p[0] == p[1] else prod[p]
                value = g * value
                if t > 1:
                    value = tensor[i, pl.ds(plane * rows, rows), :] + value
                tensor[i, pl.ds(plane * rows, rows), :] = value
            if t == steps:
                for i in range(3):
                    e_out[i, plane] = e[i]
                    h_out[i, plane] = h[i]

    def halves(v):
        high = v.astype(jnp.bfloat16)
        return high, (v - high.astype(jnp.float32)).astype(jnp.bfloat16)

    cells = planes * rows
    high, low = halves(tensor[...].reshape(len(PAIRS) * cells, lanes))
    lhs = jnp.concatenate([high, low], 1)
    slots = cell_ref.shape[1]
    owners = part_out.shape[0]
    chunk = 256
    total = jnp.zeros((2 * owners * 8, TILE_DEV), jnp.float32)
    for at in range(0, slots, chunk):
        cell = cell_ref[:, at : at + chunk]
        owner = owner_ref[:, at : at + chunk]
        normal = normal_ref[:, at : at + chunk]
        tile = tile_ref[:, at : at + chunk]
        live = (at + lax.broadcasted_iota(jnp.int32, (1, chunk), 1)) < count_ref[0, 0, 0]
        hot = jnp.where(lax.broadcasted_iota(jnp.int32, (lanes, chunk), 0) == cell % lanes, 1.0, 0.0).astype(jnp.bfloat16)
        picked = jnp.dot(lhs, jnp.concatenate([hot, hot], 0), preferred_element_type=jnp.float32)
        in_row = lax.broadcasted_iota(jnp.int32, (cells, chunk), 0) == cell // lanes
        vals = {
            p: jnp.sum(jnp.where(in_row, picked[i * cells : (i + 1) * cells], 0.0), axis=0, keepdims=True)
            for i, p in enumerate(PAIRS)
        }
        axis = normal // 2
        sign = (1 - 2 * (normal % 2)).astype(jnp.float32)
        scale = jnp.where(live, FACE_AREA * sign, 0.0)
        row_force = []
        for i in range(3):
            by = [vals[min(i, a), max(i, a)] for a in range(3)]
            row_force.append(scale * jnp.where(axis == 0, by[0], jnp.where(axis == 1, by[1], by[2])))
        stacked = jnp.concatenate(row_force + [jnp.zeros((5, chunk), jnp.float32)], 0)
        spread = jnp.concatenate([jnp.where(owner == o, stacked, 0.0) for o in range(owners)], 0)
        a_high, a_low = halves(spread)
        a = jnp.concatenate([a_high, a_low], 0)
        tile_hot = jnp.where(lax.broadcasted_iota(jnp.int32, (TILE_DEV, chunk), 0) == tile, 1.0, 0.0).astype(jnp.bfloat16)
        total = total + lax.dot_general(a, tile_hot, (((1,), (1,)), ((), ())), preferred_element_type=jnp.float32)
    part = total[: owners * 8] + total[owners * 8 :]
    for o in range(owners):
        part_out[o] = part[o * 8 : (o + 1) * 8]


def local(sizes, e_field, h_field, current, material, sigma_table, gamma_table, plasma_table, g_kernel,
          surf_cell, surf_owner, surf_tile, surf_normal, row_count):
    n_x, n_y, n_z = sizes
    steps = g_kernel.shape[0]
    planes, rows, lanes = material.shape
    f32 = jnp.float32
    n_msg = 10 * planes
    z_tiles = -(-n_msg * steps // lanes)
    brick, z_first, z_second = pl.pallas_call(
        functools.partial(pack_kernel, steps),
        out_shape=(
            jax.ShapeDtypeStruct((n_msg, rows, lanes), f32),
            jax.ShapeDtypeStruct((z_tiles, rows, lanes), f32),
            jax.ShapeDtypeStruct((z_tiles, rows, lanes), f32),
        ),
        in_specs=[VMEM] * 4,
        out_specs=(VMEM,) * 3,
        compiler_params=pltpu.CompilerParams(vmem_limit_bytes=4 << 20),
        name="pack",
    )(e_field, h_field, current, material)

    def send(value, axis, second=False):
        return lax.ppermute(value, AXES, full_swap(sizes, axis, second))

    x_first, x_second = send(brick, "gx"), send(brick, "gx", True)
    z_first, z_second = send(z_first, "gz"), send(z_second, "gz", True)
    parts = [
        brick,
        x_first,
        x_second,
        z_first,
        z_second,
        send(z_first, "gx"),
        send(z_second, "gx"),
        send(z_first, "gx", True),
        send(z_second, "gx", True),
    ]
    counts = [p.shape[0] for p in parts]
    n_ghost = 1 if n_y == 2 else 2
    outgoing = pl.pallas_call(
        functools.partial(rows_kernel, len(parts), n_y),
        out_shape=[jax.ShapeDtypeStruct((sum(counts), 8, lanes), f32)] * n_ghost,
        in_specs=[VMEM] * len(parts),
        out_specs=[VMEM] * n_ghost,
        compiler_params=pltpu.CompilerParams(vmem_limit_bytes=6 << 20),
        name="rows",
    )(*parts)
    ghosts = [send(v, "gy", bool(i)) for i, v in enumerate(outgoing)]

    owners = n_x * n_y
    slots = surf_cell.size
    wide = 2 * lanes
    e_out, h_out, part = pl.pallas_call(
        functools.partial(main_kernel, sizes, steps, sigma_table.shape[0], counts),
        out_shape=(
            jax.ShapeDtypeStruct(e_field.shape, f32),
            jax.ShapeDtypeStruct(h_field.shape, f32),
            jax.ShapeDtypeStruct((owners, 8, TILE_DEV), f32),
        ),
        in_specs=[VMEM] * (len(parts) + n_ghost) + [SMEM] * 5 + [VMEM] * 4,
        out_specs=(VMEM,) * 3,
        scratch_shapes=[
            pltpu.VMEM((10, 3 * planes, rows + 8, wide), f32),
            pltpu.VMEM((4, 3 * planes, rows + 8, wide), f32),
            pltpu.VMEM((2, rows + 8, wide), f32),
            pltpu.VMEM((len(PAIRS), planes * rows, lanes), f32),
        ],
        compiler_params=pltpu.CompilerParams(vmem_limit_bytes=24 << 20),
        name="march",
    )(*parts, *ghosts, sigma_table, gamma_table, plasma_table, g_kernel, row_count,
      surf_cell.reshape(1, slots), surf_owner.reshape(1, slots), surf_tile.reshape(1, slots), surf_normal.reshape(1, slots))
    got = lax.all_to_all(part, ("gx", "gy"), split_axis=0, concat_axis=0, tiled=True)
    force = jnp.sum(got[:, :3], axis=0)
    return e_out, h_out, force


def solution(mesh):
    sizes = tuple(mesh.shape[a] for a in AXES)
    return jax.shard_map(
        functools.partial(local, sizes),
        mesh=mesh,
        in_specs=(
            P(None, "gx", "gy", "gz"),
            P(None, "gx", "gy", "gz"),
            P(None, "gx", "gy", "gz"),
            P("gx", "gy", "gz"),
            P(),
            P(),
            P(),
            P(),
            P("gx", "gy", "gz", None),
            P("gx", "gy", "gz", None, None),
            P("gx", "gy", "gz", None),
            P("gx", "gy", "gz", None),
            P("gx", "gy", "gz"),
        ),
        out_specs=(
            P(None, "gx", "gy", "gz"),
            P(None, "gx", "gy", "gz"),
            P(None, ("gx", "gy", "gz")),
        ),
        check_vma=False,
    )
```

```python
import functools

import jax
import jax.numpy as jnp
from jax import lax
from jax.experimental import pallas as pl
from jax.experimental.pallas import tpu as pltpu
from jax.sharding import PartitionSpec as P

STEP_DT = 0.5
FACE_AREA = 0.25
TILE_DEV = 128
PAIRS = ((0, 0), (0, 1), (0, 2), (1, 1), (1, 2), (2, 2))
AXES = ("gx", "gy", "gz")
VMEM = pl.BlockSpec(memory_space=pltpu.VMEM)
SMEM = pl.BlockSpec(memory_space=pltpu.SMEM)


def partner(index, size, second):
    if not second:
        return index ^ 1
    return (index - 1) % size if index % 2 == 0 else (index + 1) % size


def full_swap(sizes, axis, second=False):
    pairs = []
    at = AXES.index(axis)
    for x in range(sizes[0]):
        for y in range(sizes[1]):
            for z in range(sizes[2]):
                to = [x, y, z]
                if second and to[at] in (0, sizes[at] - 1) and axis != "gy":
                    to[1] = y ^ 1
                else:
                    to[at] = partner(to[at], sizes[at], second)
                pairs.append(((x * sizes[1] + y) * sizes[2] + z, (to[0] * sizes[1] + to[1]) * sizes[2] + to[2]))
    return pairs


def pack_kernel(depth, e_ref, h_ref, j_ref, m_ref, brick_ref, even_ref, odd_ref, m_buf, sems):
    planes, rows, lanes = m_ref.shape
    count = 3 * planes
    copies = [pltpu.make_async_copy(ref, brick_ref.at[pl.ds(i * count, count)], sems.at[i]) for i, ref in enumerate((e_ref, h_ref, j_ref))]
    copies.append(pltpu.make_async_copy(m_ref, m_buf, sems.at[3]))
    for copy in copies:
        copy.start()
    per_tile = lanes // depth
    group = lax.broadcasted_iota(jnp.int32, (rows, lanes), 1) // depth
    tiles = even_ref.shape[0]
    low = [jnp.zeros((rows, lanes), jnp.float32) for _ in range(tiles)]
    high = [jnp.zeros((rows, lanes), jnp.float32) for _ in range(tiles)]
    for j in range(3 * count + planes):
        if j % count == 0:
            copies[j // count].wait()
        if j >= 3 * count:
            brick_ref[j] = (m_buf[j - 3 * count] + 1).astype(jnp.float32)
        value = brick_ref[j]
        tile, slot = j // per_tile, j % per_tile
        up = pltpu.roll(value, depth * slot, 1) if slot else value
        down = pltpu.roll(value, lanes - depth * slot, 1) if slot else value
        low[tile] = jnp.where(group == slot, up, low[tile])
        high[tile] = jnp.where(group == per_tile - 1 - slot, down, high[tile])
    is_even = lax.axis_index("gz") % 2 == 0
    for tile in range(tiles):
        even_ref[tile] = jnp.where(is_even, high[tile], low[tile])
        odd_ref[tile] = jnp.where(is_even, low[tile], high[tile])


def prepare_kernel(materials, steps, cells, lanes, sigma_ref, gamma_ref, plasma_ref, g_ref, count_ref,
                   cell_ref, owner_ref, tile_ref, normal_ref, after_ref,
                   table_ref, hot_ref, tile_hot_ref, ints_ref, scale_ref):
    del after_ref
    slots = cell_ref.shape[1]
    shape = table_ref.shape[1:]

    def splat(value):
        return jnp.full(shape, value, jnp.float32)

    for which in range(materials):
        sigma, gamma, plasma = splat(sigma_ref[which]), splat(gamma_ref[which]), splat(plasma_ref[which])
        table_ref[4 * which] = (1.0 - sigma * STEP_DT / 2) / (1.0 + sigma * STEP_DT / 2)
        table_ref[4 * which + 1] = STEP_DT / (1.0 + sigma * STEP_DT / 2)
        table_ref[4 * which + 2] = (1.0 - gamma * STEP_DT / 2) / (1.0 + gamma * STEP_DT / 2)
        table_ref[4 * which + 3] = plasma * STEP_DT / (1.0 + gamma * STEP_DT / 2)
    for t in range(steps):
        table_ref[4 * materials + t] = splat(g_ref[t])
    cell, normal = cell_ref[...], normal_ref[...]
    in_lane, in_row = cell % lanes, cell // lanes
    hot = lax.broadcasted_iota(jnp.int32, (lanes, slots), 0) == in_lane
    hot_ref[...] = jnp.where(hot, 1.0, 0.0).astype(jnp.bfloat16)
    tile_hot = lax.broadcasted_iota(jnp.int32, (TILE_DEV, slots), 0) == tile_ref[...]
    tile_hot_ref[...] = jnp.where(tile_hot, 1.0, 0.0).astype(jnp.bfloat16)
    ints_ref[0:1] = in_row
    ints_ref[1:2] = owner_ref[...]
    ints_ref[2:3] = normal // 2
    live = lax.broadcasted_iota(jnp.int32, (1, slots), 1) < count_ref[0]
    sign = (1 - 2 * (normal % 2)).astype(jnp.float32)
    scale_ref[...] = jnp.where(live, FACE_AREA * sign, 0.0)


def rows_kernel(n_in, *refs):
    ins, outs = refs[:n_in], refs[n_in + 1 :]
    is_odd = lax.axis_index("gy") % 2
    at = 0
    for ref in ins:
        count, rows, _ = ref.shape
        for which, out in enumerate(outs):
            last = (1 - is_odd) if which == 0 else is_odd
            start = pl.multiple_of(last * (rows - 8), 8)
            out[pl.ds(at, count)] = ref[:, pl.ds(start, 8), :]
        at += count


def main_kernel(sizes, steps, materials, counts, *refs):
    n_x, n_y, n_z = sizes
    n_in = len(counts)
    n_ghost = 1 if n_y == 2 else 2
    parts, refs = refs[:n_in], refs[n_in:]
    ghosts, refs = refs[:n_ghost], refs[n_ghost:]
    table_ref, hot_ref, tile_hot_ref, ints_ref, scale_ref = refs[:5]
    e_out, h_out, part_out = refs[5:8]
    field, coef, gain_h, tensor = refs[8:12]
    _, rows, lanes = parts[0].shape
    planes = e_out.shape[1]
    depth = steps
    per_tile = lanes // depth
    x, y, z = (lax.axis_index(a) for a in AXES)
    even_x, even_y, even_z = x % 2 == 0, y % 2 == 0, z % 2 == 0
    low_x, high_x = x > 0, x < n_x - 1
    low_y, high_y = y > 0, y < n_y - 1
    low_z, high_z = z > 0, z < n_z - 1
    row8 = lax.broadcasted_iota(jnp.int32, (8, lanes), 0)
    lower_from = jnp.where(low_y, 8 - depth, 8)
    upper_to = jnp.where(high_y, depth, 0)
    lower_rows = row8 >= lower_from
    upper_rows = row8 < upper_to
    one_side = (row8 >= jnp.where(even_y, 0, lower_from)) & (row8 < jnp.where(even_y, upper_to, 8))

    offsets = [sum(counts[:i]) for i in range(n_in)]

    def ghost_rows(at):
        if n_ghost == 1:
            value = ghosts[0][at]
            return jnp.where(one_side, value, 0.0)
        first, second = ghosts[0][at], ghosts[1][at]
        upper = jnp.where(even_y, first, second)
        lower = jnp.where(even_y, second, first)
        return jnp.where(upper_rows, upper, jnp.where(lower_rows, lower, 0.0))

    def whole(part, j):
        return jnp.concatenate([parts[part][j], ghost_rows(offsets[part] + j)], 0)

    full_rows = rows + 8
    lane = lax.broadcasted_iota(jnp.int32, (full_rows, lanes), 1)
    upper_lanes = lane < jnp.where(high_z, depth, 0)
    lower_lanes = lane >= jnp.where(low_z, lanes - depth, lanes)
    n_fields = 10
    z_tiles = counts[3] // 2

    def edges(part):
        out = []
        for tile in range(z_tiles):
            first, second = whole(part, tile), whole(part, z_tiles + tile)
            out.append((jnp.where(even_z, first, second), jnp.where(even_z, second, first)))
        return out

    own_edges, first_edges, second_edges = edges(3), edges(4), edges(5)
    for cls in range(3):
        for j in range(n_fields * planes):
            tile, slot = j // per_tile, j % per_tile
            if cls == 1:
                main = whole(0, j)
                upper, lower = own_edges[tile]
            else:
                first, second = whole(1, j), whole(2, j)
                take_first = even_x if cls == 2 else jnp.logical_not(even_x)
                valid = high_x if cls == 2 else low_x
                main = jnp.where(valid, jnp.where(take_first, first, second), 0.0)
                upper = jnp.where(valid, jnp.where(take_first, first_edges[tile][0], second_edges[tile][0]), 0.0)
                lower = jnp.where(valid, jnp.where(take_first, first_edges[tile][1], second_edges[tile][1]), 0.0)
            if slot:
                upper = pltpu.roll(upper, lanes - depth * slot, 1)
                lower = pltpu.roll(lower, depth * slot, 1)
            side = jnp.where(upper_lanes, upper, jnp.where(lower_lanes, lower, 0.0))
            at = cls * planes + j % planes
            field[j // planes, at, :, :lanes] = main
            field[j // planes, at, :, lanes:] = side

    wide = 2 * lanes

    table = [[table_ref[4 * m + i] for i in range(4)] for m in range(materials)]
    for plane in range(1, 3 * planes - 1):
        for r in range(0, full_rows, 8):
            for c in range(0, wide, lanes):
                code = field[9, plane, r : r + 8, c : c + lanes]
                for which in range(4):
                    value = jnp.zeros((8, lanes), jnp.float32)
                    for m in range(materials):
                        value = jnp.where(code == float(m + 1), table[m][which], value)
                    coef[which, plane, r : r + 8, c : c + lanes] = value

    row = lax.broadcasted_iota(jnp.int32, (full_rows, wide), 0)
    col = lax.broadcasted_iota(jnp.int32, (full_rows, wide), 1)
    inside = (row < jnp.where(low_y, full_rows, full_rows - depth)) & (col < jnp.where(low_z, wide, wide - depth))
    gain = jnp.where(inside, STEP_DT, 0.0)
    gain_h[1] = gain
    gain_h[0] = jnp.where(low_x, gain, 0.0)

    def next_y(v):
        return pltpu.roll(v, full_rows - 1, 0)

    def next_z(v):
        return pltpu.roll(v, wide - 1, 1)

    def prev_y(v):
        return pltpu.roll(v, 1, 0)

    def prev_z(v):
        return pltpu.roll(v, 1, 1)

    last = 3 * planes - 1
    for t in range(1, steps + 1):
        for plane in range(t - 1, last - t + 1):
            ex, ey, ez = field[0, plane], field[1, plane], field[2, plane]
            hx, hy, hz = field[3, plane], field[4, plane], field[5, plane]
            ey_x, ez_x = field[1, plane + 1], field[2, plane + 1]
            dt = gain_h[0 if plane < planes else 1]
            hy = hy - dt * ((next_z(ex) - ex) - (ez_x - ez))
            hz = hz - dt * ((ey_x - ey) - (next_y(ex) - ex))
            field[4, plane] = hy
            field[5, plane] = hz
            if plane < t:
                continue
            hx = hx - dt * ((next_y(ez) - ez) - (next_z(ey) - ey))
            field[3, plane] = hx
            hy_x, hz_x = field[4, plane - 1], field[5, plane - 1]
            keep_e, gain_e, keep_j, gain_j = (coef[i, plane] for i in range(4))
            curl_x = (hz - prev_y(hz)) - (hy - prev_z(hy))
            curl_y = (hx - prev_z(hx)) - (hz - hz_x)
            curl_z = (hy - hy_x) - (hx - prev_y(hx))
            for comp, (old, curl) in enumerate(((ex, curl_x), (ey, curl_y), (ez, curl_z))):
                drude = keep_j * field[6 + comp, plane] + gain_j * old
                field[6 + comp, plane] = drude
                field[comp, plane] = keep_e * old + gain_e * (curl - drude)
        g = table_ref[4 * materials + t - 1]
        g = jnp.concatenate([g] * (rows // 8), 0)
        for plane in range(planes):
            e = [field[i, planes + plane, :rows, :lanes] for i in range(3)]
            h = [field[3 + i, planes + plane, :rows, :lanes] for i in range(3)]
            prod = {p: e[p[0]] * e[p[1]] + h[p[0]] * h[p[1]] for p in PAIRS}
            energy = 0.5 * (prod[0, 0] + prod[1, 1] + prod[2, 2])
            for i, p in enumerate(PAIRS):
                value = prod[p] - energy if p[0] == p[1] else prod[p]
                value = g * value
                if t > 1:
                    value = tensor[i, pl.ds(plane * rows, rows), :] + value
                tensor[i, pl.ds(plane * rows, rows), :] = value
            if t == steps:
                for i in range(3):
                    e_out[i, plane] = e[i]
                    h_out[i, plane] = h[i]

    def halves(v):
        high = v.astype(jnp.bfloat16)
        return high, (v - high.astype(jnp.float32)).astype(jnp.bfloat16)

    cells = planes * rows
    high, low = halves(tensor[...].reshape(len(PAIRS) * cells, lanes))
    lhs = jnp.concatenate([high, low], 1)
    slots = hot_ref.shape[1]
    owners = part_out.shape[0]
    chunk = 256
    total = jnp.zeros((2 * owners * 8, TILE_DEV), jnp.float32)
    for at in range(0, slots, chunk):
        here = slice(at, at + chunk)
        in_row, owner, axis = ints_ref[0:1, here], ints_ref[1:2, here], ints_ref[2:3, here]
        hot = hot_ref[:, here]
        picked = jnp.dot(lhs, jnp.concatenate([hot, hot], 0), preferred_element_type=jnp.float32)
        in_row = lax.broadcasted_iota(jnp.int32, (cells, chunk), 0) == in_row
        vals = {
            p: jnp.sum(jnp.where(in_row, picked[i * cells : (i + 1) * cells], 0.0), axis=0, keepdims=True)
            for i, p in enumerate(PAIRS)
        }
        row_force = []
        for i in range(3):
            by = [vals[min(i, a), max(i, a)] for a in range(3)]
            row_force.append(scale_ref[:, here] * jnp.where(axis == 0, by[0], jnp.where(axis == 1, by[1], by[2])))
        stacked = jnp.concatenate(row_force + [jnp.zeros((5, chunk), jnp.float32)], 0)
        spread = jnp.concatenate([jnp.where(owner == o, stacked, 0.0) for o in range(owners)], 0)
        a_high, a_low = halves(spread)
        a = jnp.concatenate([a_high, a_low], 0)
        total = total + lax.dot_general(a, tile_hot_ref[:, here], (((1,), (1,)), ((), ())), preferred_element_type=jnp.float32)
    part = total[: owners * 8] + total[owners * 8 :]
    for o in range(owners):
        part_out[o] = part[o * 8 : (o + 1) * 8]


def local(sizes, e_field, h_field, current, material, sigma_table, gamma_table, plasma_table, g_kernel,
          surf_cell, surf_owner, surf_tile, surf_normal, row_count):
    n_x, n_y, n_z = sizes
    steps = g_kernel.shape[0]
    planes, rows, lanes = material.shape
    f32 = jnp.float32
    n_msg = 10 * planes
    z_tiles = -(-n_msg * steps // lanes)
    brick, z_first, z_second = pl.pallas_call(
        functools.partial(pack_kernel, steps),
        out_shape=(
            jax.ShapeDtypeStruct((n_msg, rows, lanes), f32),
            jax.ShapeDtypeStruct((z_tiles, rows, lanes), f32),
            jax.ShapeDtypeStruct((z_tiles, rows, lanes), f32),
        ),
        in_specs=[pl.BlockSpec(memory_space=pltpu.HBM)] * 4,
        out_specs=(VMEM,) * 3,
        scratch_shapes=[pltpu.VMEM((planes, rows, lanes), jnp.int32), pltpu.SemaphoreType.DMA((4,))],
        compiler_params=pltpu.CompilerParams(vmem_limit_bytes=4 << 20),
        name="pack",
    )(*(pltpu.with_memory_space_constraint(v, pltpu.HBM) for v in (
        e_field.reshape(3 * planes, rows, lanes), h_field.reshape(3 * planes, rows, lanes),
        current.reshape(3 * planes, rows, lanes), material)))

    def send(value, axis, second=False):
        return lax.ppermute(value, AXES, full_swap(sizes, axis, second))

    x_first, x_second = send(brick, "gx"), send(brick, "gx", True)
    edges = jnp.concatenate([send(z_first, "gz"), send(z_second, "gz", True)])
    parts = [brick, x_first, x_second, edges, send(edges, "gx"), send(edges, "gx", True)]

    slots = surf_cell.size
    materials = sigma_table.shape[0]
    prepared = pl.pallas_call(
        functools.partial(prepare_kernel, materials, steps, planes * rows, lanes),
        out_shape=(
            jax.ShapeDtypeStruct((4 * materials + steps, 8, lanes), f32),
            jax.ShapeDtypeStruct((lanes, slots), jnp.bfloat16),
            jax.ShapeDtypeStruct((TILE_DEV, slots), jnp.bfloat16),
            jax.ShapeDtypeStruct((8, slots), jnp.int32),
            jax.ShapeDtypeStruct((1, slots), f32),
        ),
        in_specs=[SMEM] * 4 + [VMEM] * 5 + [pl.BlockSpec(memory_space=pl.ANY)],
        out_specs=(VMEM,) * 5,
        compiler_params=pltpu.CompilerParams(vmem_limit_bytes=6 << 20),
        cost_estimate=pl.CostEstimate(flops=1 << 20, bytes_accessed=1 << 20, transcendentals=0),
        name="prepare",
    )(sigma_table, gamma_table, plasma_table, g_kernel, row_count,
      surf_cell.reshape(1, slots), surf_owner.reshape(1, slots), surf_tile.reshape(1, slots), surf_normal.reshape(1, slots), edges)
    counts = [p.shape[0] for p in parts]
    n_ghost = 1 if n_y == 2 else 2
    outgoing = pl.pallas_call(
        functools.partial(rows_kernel, len(parts)),
        out_shape=[jax.ShapeDtypeStruct((sum(counts), 8, lanes), f32)] * n_ghost,
        in_specs=[VMEM] * len(parts) + [pl.BlockSpec(memory_space=pl.ANY)],
        out_specs=[VMEM] * n_ghost,
        compiler_params=pltpu.CompilerParams(vmem_limit_bytes=6 << 20),
        name="rows",
    )(*parts, prepared[-1])
    ghosts = [send(v, "gy", bool(i)) for i, v in enumerate(outgoing)]

    owners = n_x * n_y
    wide = 2 * lanes
    e_out, h_out, part = pl.pallas_call(
        functools.partial(main_kernel, sizes, steps, sigma_table.shape[0], counts),
        out_shape=(
            jax.ShapeDtypeStruct(e_field.shape, f32),
            jax.ShapeDtypeStruct(h_field.shape, f32),
            jax.ShapeDtypeStruct((owners, 8, TILE_DEV), f32),
        ),
        in_specs=[VMEM] * (len(parts) + n_ghost + len(prepared)),
        out_specs=(VMEM,) * 3,
        scratch_shapes=[
            pltpu.VMEM((10, 3 * planes, rows + 8, wide), f32),
            pltpu.VMEM((4, 3 * planes, rows + 8, wide), f32),
            pltpu.VMEM((2, rows + 8, wide), f32),
            pltpu.VMEM((len(PAIRS), planes * rows, lanes), f32),
        ],
        compiler_params=pltpu.CompilerParams(vmem_limit_bytes=24 << 20),
        name="march",
    )(*parts, *ghosts, *prepared)
    got = lax.all_to_all(part, ("gx", "gy"), split_axis=0, concat_axis=0, tiled=True)
    force = jnp.sum(got[:, :3], axis=0)
    return e_out, h_out, force


def solution(mesh):
    sizes = tuple(mesh.shape[a] for a in AXES)
    return jax.shard_map(
        functools.partial(local, sizes),
        mesh=mesh,
        in_specs=(
            P(None, "gx", "gy", "gz"),
            P(None, "gx", "gy", "gz"),
            P(None, "gx", "gy", "gz"),
            P("gx", "gy", "gz"),
            P(),
            P(),
            P(),
            P(),
            P("gx", "gy", "gz", None),
            P("gx", "gy", "gz", None, None),
            P("gx", "gy", "gz", None),
            P("gx", "gy", "gz", None),
            P("gx", "gy", "gz"),
        ),
        out_specs=(
            P(None, "gx", "gy", "gz"),
            P(None, "gx", "gy", "gz"),
            P(None, ("gx", "gy", "gz")),
        ),
        check_vma=False,
    )
```

```python
import functools

import jax
import jax.numpy as jnp
from jax import lax
from jax.experimental import pallas as pl
from jax.experimental.pallas import tpu as pltpu
from jax.sharding import PartitionSpec as P


STEP_DT = 0.5
FACE_AREA = 0.25
TILE_DEV = 128
PAIRS = ((0, 0), (0, 1), (0, 2), (1, 1), (1, 2), (2, 2))
AXES = ("gx", "gy", "gz")
VMEM = pl.BlockSpec(memory_space=pltpu.VMEM)
SMEM = pl.BlockSpec(memory_space=pltpu.SMEM)


def partner(index, size, second):
    if not second:
        return index ^ 1
    return (index - 1) % size if index % 2 == 0 else (index + 1) % size


def full_swap(sizes, axis, second=False):
    pairs = []
    at = AXES.index(axis)
    for x in range(sizes[0]):
        for y in range(sizes[1]):
            for z in range(sizes[2]):
                to = [x, y, z]
                if second and to[at] in (0, sizes[at] - 1) and axis != "gy":
                    to[1] = y ^ 1
                else:
                    to[at] = partner(to[at], sizes[at], second)
                pairs.append(((x * sizes[1] + y) * sizes[2] + z, (to[0] * sizes[1] + to[1]) * sizes[2] + to[2]))
    return pairs


def pack_kernel(depth, n_ghost, *refs):
    e_ref, h_ref, j_ref, m_ref = refs[:4]
    n_small = (len(refs) - 4 - 4 - n_ghost) // 2
    small, refs = refs[4 : 4 + n_small], refs[4 + n_small :]
    brick_ref, edge_ref, refs = refs[0], refs[1], refs[2:]
    sends, kept, (m_buf, sems) = refs[:n_ghost], refs[n_ghost : n_ghost + n_small], refs[n_ghost + n_small :]
    planes, rows, lanes = m_ref.shape
    count = 3 * planes
    copies = [pltpu.make_async_copy(ref, brick_ref.at[pl.ds(i * count, count)], sems.at[i]) for i, ref in enumerate((e_ref, h_ref, j_ref))]
    copies.append(pltpu.make_async_copy(m_ref, m_buf, sems.at[3]))
    copies += [pltpu.make_async_copy(src, dst, sems.at[4 + i]) for i, (src, dst) in enumerate(zip(small, kept, strict=True))]
    for copy in copies:
        copy.start()
    width = 2 * depth * planes
    per_tile = lanes // width
    lane = lax.broadcasted_iota(jnp.int32, (rows, lanes), 1)
    packed = [jnp.zeros((rows, lanes), jnp.float32) for _ in range(edge_ref.shape[0])]
    for j in range(3 * count + planes):
        if j % count == 0:
            copies[j // count].wait()
        if j >= 3 * count:
            brick_ref[j] = (m_buf[j - 3 * count] + 1).astype(jnp.float32)
        value = brick_ref[j]
        tile, start = j // planes // per_tile, j // planes % per_tile * width + j % planes * 2 * depth
        turned = pltpu.roll(value, (start + depth) % lanes, 1)
        packed[tile] = jnp.where((lane >= start) & (lane < start + 2 * depth), turned, packed[tile])
    is_odd = lax.axis_index("gy") % 2 == 1
    for tile, value in enumerate(packed):
        edge_ref[tile] = value
        first, last = value[:8], value[rows - 8 :]
        sends[0][tile] = jnp.where(is_odd, first, last)
        if n_ghost > 1:
            sends[1][tile] = jnp.where(is_odd, last, first)
    for copy in copies[4:]:
        copy.wait()


def sides_y(depth, n_y, lanes):
    y = lax.axis_index("gy")
    even = y % 2 == 0
    row = lax.broadcasted_iota(jnp.int32, (8, lanes), 0)
    upper_to = jnp.where(y < n_y - 1, depth, 0)
    lower_from = jnp.where(y > 0, 8 - depth, 8)

    def pick(values):
        if len(values) == 1:
            wanted = (row >= jnp.where(even, 0, lower_from)) & (row < jnp.where(even, upper_to, 8))
            return jnp.where(wanted, values[0], 0.0)
        upper = jnp.where(even, values[0], values[1])
        lower = jnp.where(even, values[1], values[0])
        return jnp.where(row < upper_to, upper, jnp.where(row >= lower_from, lower, 0.0))

    return pick


def widen_kernel(depth, n_y, edge_ref, *refs):
    ghosts, out = refs[:-1], refs[-1]
    pick = sides_y(depth, n_y, edge_ref.shape[2])
    rows = edge_ref.shape[1]
    for tile in range(edge_ref.shape[0]):
        out[tile, :rows] = edge_ref[tile]
        out[tile, rows:] = pick([g[tile] for g in ghosts])


def merge_kernel(depth, n_z, first_ref, second_ref, out_ref):
    z = lax.axis_index("gz")
    even = z % 2 == 0
    shape = out_ref.shape[1:]
    place = lax.broadcasted_iota(jnp.int32, shape, 1) % (2 * depth)
    is_lower = place < jnp.where(z > 0, depth, 0)
    is_upper = place >= jnp.where(z < n_z - 1, depth, 2 * depth)
    for tile in range(out_ref.shape[0]):
        first, second = first_ref[tile], second_ref[tile]
        upper = jnp.where(even, first, second)
        lower = jnp.where(even, second, first)
        out_ref[tile] = jnp.where(is_upper, upper, jnp.where(is_lower, lower, 0.0))


def rows_kernel(depth, n_in, *refs):
    ins, outs = refs[:n_in], refs[n_in + 1 :]
    is_odd = lax.axis_index("gy") % 2
    row = lax.broadcasted_iota(jnp.int32, (8, outs[0].shape[2]), 0)
    at = 0
    for ref in ins:
        count, rows, _ = ref.shape
        for which, out in enumerate(outs):
            last = (1 - is_odd) if which == 0 else is_odd
            start = pl.multiple_of(last * (rows - 8), 8)
            mine = (row >= jnp.where(last == 1, 8 - depth, 0)) & (row < jnp.where(last == 1, 8, depth))
            for j in range(0, count, 2):
                kept, turned = ref[j, pl.ds(start, 8), :], ref[j + 1, pl.ds(start, 8), :]
                out[(at + j) // 2] = jnp.where(mine, kept, pltpu.roll(turned, 4, 0))
        at += count


def prepare_kernel(materials, steps, lanes, sigma_ref, gamma_ref, plasma_ref, g_ref,
                   cell_ref, owner_ref, tile_ref, normal_ref, count_ref, after_ref,
                   table_ref, hot_ref, tile_hot_ref, ints_ref, scale_ref):
    del after_ref
    slots = cell_ref.shape[1]
    shape = table_ref.shape[1:]

    def splat(ref, at):
        return jnp.broadcast_to(ref[:, at : at + 1], shape)

    for which in range(materials):
        sigma, gamma, plasma = splat(sigma_ref, which), splat(gamma_ref, which), splat(plasma_ref, which)
        table_ref[4 * which] = (1.0 - sigma * STEP_DT / 2) / (1.0 + sigma * STEP_DT / 2)
        table_ref[4 * which + 1] = STEP_DT / (1.0 + sigma * STEP_DT / 2)
        table_ref[4 * which + 2] = (1.0 - gamma * STEP_DT / 2) / (1.0 + gamma * STEP_DT / 2)
        table_ref[4 * which + 3] = plasma * STEP_DT / (1.0 + gamma * STEP_DT / 2)
    for t in range(steps):
        table_ref[4 * materials + t] = splat(g_ref, t)
    cell, normal = cell_ref[...], normal_ref[...]
    in_lane, in_row = cell % lanes, cell // lanes
    hot = lax.broadcasted_iota(jnp.int32, (lanes, slots), 0) == in_lane
    hot_ref[...] = jnp.where(hot, 1.0, 0.0).astype(jnp.bfloat16)
    tile_hot = lax.broadcasted_iota(jnp.int32, (TILE_DEV, slots), 0) == tile_ref[...]
    tile_hot_ref[...] = jnp.where(tile_hot, 1.0, 0.0).astype(jnp.bfloat16)
    ints_ref[0:1] = in_row
    ints_ref[1:2] = owner_ref[...]
    ints_ref[2:3] = normal // 2
    live = lax.broadcasted_iota(jnp.int32, (1, slots), 1) < count_ref[0, 0, 0]
    sign = (1 - 2 * (normal % 2)).astype(jnp.float32)
    scale_ref[...] = jnp.where(live, FACE_AREA * sign, 0.0)


def main_kernel(sizes, steps, materials, n_ghost, *refs):
    n_x, n_y, _ = sizes
    bricks, ghosts, refs = refs[:3], refs[3 : 3 + n_ghost], refs[3 + n_ghost :]
    edge_refs, refs = refs[:3], refs[3:]
    table_ref, hot_ref, tile_hot_ref, ints_ref, scale_ref = refs[:5]
    e_out, h_out, part_out = refs[5:8]
    field, coef, side, side_coef, tensor = refs[8:13]
    n_msg, rows, lanes = bricks[0].shape
    planes = e_out.shape[1]
    depth = steps
    x, y, z = (lax.axis_index(a) for a in AXES)
    even_x = x % 2 == 0
    low_x, high_x, low_y, low_z = x > 0, x < n_x - 1, y > 0, z > 0
    pick = sides_y(depth, n_y, lanes)
    full = rows + 8

    def whole(which, j):
        at = which * n_msg + j
        values = [g[at // 2] for g in ghosts]
        if at % 2:
            values = [pltpu.roll(v, 4, 0) for v in values]
        return jnp.concatenate([bricks[which][j], pick(values)], 0)

    for j in range(n_msg):
        f, p = j // planes, j % planes
        first, second = whole(1, j), whole(2, j)
        field[f, planes + p] = whole(0, j)
        field[f, p] = jnp.where(low_x, jnp.where(even_x, second, first), 0.0)
        field[f, 2 * planes + p] = jnp.where(high_x, jnp.where(even_x, first, second), 0.0)

    width = 2 * depth * planes
    per_tile = lanes // width
    lane = lax.broadcasted_iota(jnp.int32, (full, lanes), 1)
    at_low = lane < jnp.where(low_x, width, 0)
    at_own = (lane >= width) & (lane < 2 * width)
    at_high = (lane >= 2 * width) & (lane < jnp.where(high_x, 3 * width, 0))
    tiles = []
    for tile in range(edge_refs[0].shape[0]):
        own, first, second = (r[tile] for r in edge_refs)
        tiles.append((jnp.where(even_x, second, first), own, jnp.where(even_x, first, second)))
    for f in range(n_msg // planes):
        start = f % per_tile * width
        low, own, high = (
            pltpu.roll(v, (cls * width - start) % lanes, 1) if cls * width != start else v
            for cls, v in enumerate(tiles[f // per_tile])
        )
        side[f] = jnp.where(at_low, low, jnp.where(at_own, own, jnp.where(at_high, high, 0.0)))

    table = [[table_ref[4 * m + i] for i in range(4)] for m in range(materials)]

    def look_up(code, which):
        value = jnp.zeros((8, lanes), jnp.float32)
        for m in range(materials):
            value = jnp.where(code == float(m + 1), table[m][which], value)
        return value

    for r in range(0, full, 8):
        for which in range(4):
            for plane in range(1, 3 * planes - 1):
                coef[which, plane, r : r + 8] = look_up(field[9, plane, r : r + 8], which)
            side_coef[which, r : r + 8] = look_up(side[9, r : r + 8], which)

    row = lax.broadcasted_iota(jnp.int32, (full, lanes), 0)
    dt_all = jnp.where(row < jnp.where(low_y, full, full - depth), STEP_DT, 0.0)
    dt_low = jnp.where(low_x, dt_all, 0.0)
    dt_side = jnp.where((lane >= jnp.where(low_x, 0, width)) & (lane < 3 * width), dt_all, 0.0)
    dt_side = jnp.where(lane % (2 * depth) >= jnp.where(low_z, 0, depth), dt_side, 0.0)

    def turn(v, by):
        by = by % lanes
        return pltpu.roll(v, by, 1) if by else v

    def next_y(v):
        return pltpu.roll(v, full - 1, 0)

    def prev_y(v):
        return pltpu.roll(v, 1, 0)

    def above(plane):
        return 2 * depth * plane + depth

    def next_z(v, ghost, plane):
        return jnp.where(lane == lanes - 1, turn(ghost, lanes - 1 - above(plane)), turn(v, -1))

    def prev_z(v, ghost, plane):
        return jnp.where(lane == 0, turn(ghost, 1 - above(plane)), turn(v, 1))

    last = 3 * planes - 1
    for t in range(1, steps + 1):
        final = t == steps
        keep_rows = rows if final else full
        h_planes = range(t - 1, last - t + 1)
        ex, ey, ez, hx, hy, hz = (side[i] for i in range(6))
        ex_z, ey_z = turn(ex, -1), turn(ey, -1)
        for plane in h_planes:
            here = lane == above(plane) - 1
            ex_z = jnp.where(here, turn(field[0, plane], above(plane) - 1), ex_z)
            ey_z = jnp.where(here, turn(field[1, plane], above(plane) - 1), ey_z)
        ey_x, ez_x = turn(ey, -2 * depth), turn(ez, -2 * depth)
        ghx = hx - dt_side * ((next_y(ez) - ez) - (ey_z - ey))
        ghy = hy - dt_side * ((ex_z - ex) - (ez_x - ez))
        ghz = hz - dt_side * ((ey_x - ey) - (next_y(ex) - ex))
        gex, gey, gez = ex, ey, ez
        hx_above, hy_above = turn(ghx, 1), turn(ghy, 1)
        for plane in h_planes:
            ex, ey, ez = field[0, plane], field[1, plane], field[2, plane]
            hx, hy, hz = field[3, plane], field[4, plane], field[5, plane]
            ey_x, ez_x = field[1, plane + 1], field[2, plane + 1]
            dt = dt_low if plane < planes else dt_all
            hy = hy - dt * ((next_z(ex, gex, plane) - ex) - (ez_x - ez))
            hz = hz - dt * ((ey_x - ey) - (next_y(ex) - ex))
            field[4, plane] = hy
            field[5, plane] = hz
            if plane < t:
                continue
            hx = hx - dt * ((next_y(ez) - ez) - (next_z(ey, gey, plane) - ey))
            field[3, plane] = hx
            if not final:
                here = lane == above(plane)
                hx_above = jnp.where(here, turn(hx, above(plane) - (lanes - 1)), hx_above)
                hy_above = jnp.where(here, turn(hy, above(plane) - (lanes - 1)), hy_above)
            hy_x, hz_x = field[4, plane - 1], field[5, plane - 1]
            curls = (
                (hz - prev_y(hz)) - (hy - prev_z(hy, ghy, plane)),
                (hx - prev_z(hx, ghx, plane)) - (hz - hz_x),
                (hy - hy_x) - (hx - prev_y(hx)),
            )
            keep_e, gain_e, keep_j, gain_j = (coef[i, plane, :keep_rows] for i in range(4))
            for comp, (old, curl) in enumerate(zip((ex, ey, ez), curls, strict=True)):
                drude = keep_j * field[6 + comp, plane, :keep_rows] + gain_j * old[:keep_rows]
                if not final:
                    field[6 + comp, plane] = drude
                field[comp, plane, :keep_rows] = keep_e * old[:keep_rows] + gain_e * (curl[:keep_rows] - drude)
        if not final:
            side[3], side[4], side[5] = ghx, ghy, ghz
            hy_x, hz_x = turn(ghy, 2 * depth), turn(ghz, 2 * depth)
            curls = (
                (ghz - prev_y(ghz)) - (ghy - hy_above),
                (ghx - hx_above) - (ghz - hz_x),
                (ghy - hy_x) - (ghx - prev_y(ghx)),
            )
            keep_e, gain_e, keep_j, gain_j = (side_coef[i] for i in range(4))
            for comp, (old, curl) in enumerate(zip((gex, gey, gez), curls, strict=True)):
                drude = keep_j * side[6 + comp] + gain_j * old
                side[6 + comp] = drude
                side[comp] = keep_e * old + gain_e * (curl - drude)
        g = table_ref[4 * materials + t - 1]
        g = jnp.concatenate([g] * (rows // 8), 0)
        for plane in range(planes):
            e = [field[i, planes + plane, :rows] for i in range(3)]
            h = [field[3 + i, planes + plane, :rows] for i in range(3)]
            prod = {p: e[p[0]] * e[p[1]] + h[p[0]] * h[p[1]] for p in PAIRS}
            energy = 0.5 * (prod[0, 0] + prod[1, 1] + prod[2, 2])
            for i, p in enumerate(PAIRS):
                value = prod[p] - energy if p[0] == p[1] else prod[p]
                value = g * value
                if t > 1:
                    value = tensor[i, pl.ds(plane * rows, rows), :] + value
                tensor[i, pl.ds(plane * rows, rows), :] = value
            if final:
                for i in range(3):
                    e_out[i, plane] = e[i]
                    h_out[i, plane] = h[i]

    def halves(v):
        high = v.astype(jnp.bfloat16)
        return high, (v - high.astype(jnp.float32)).astype(jnp.bfloat16)

    cells = planes * rows
    high, low = halves(tensor[...].reshape(len(PAIRS) * cells, lanes))
    lhs = jnp.concatenate([high, low], 1)
    slots = hot_ref.shape[1]
    owners = part_out.shape[0]
    chunk = 256
    total = jnp.zeros((2 * owners * 8, TILE_DEV), jnp.float32)
    for at in range(0, slots, chunk):
        here = slice(at, at + chunk)
        in_row, owner, axis = ints_ref[0:1, here], ints_ref[1:2, here], ints_ref[2:3, here]
        hot = hot_ref[:, here]
        picked = jnp.dot(lhs, jnp.concatenate([hot, hot], 0), preferred_element_type=jnp.float32)
        in_row = lax.broadcasted_iota(jnp.int32, (cells, chunk), 0) == in_row
        vals = {
            p: jnp.sum(jnp.where(in_row, picked[i * cells : (i + 1) * cells], 0.0), axis=0, keepdims=True)
            for i, p in enumerate(PAIRS)
        }
        row_force = []
        for i in range(3):
            by = [vals[min(i, a), max(i, a)] for a in range(3)]
            row_force.append(scale_ref[:, here] * jnp.where(axis == 0, by[0], jnp.where(axis == 1, by[1], by[2])))
        stacked = jnp.concatenate(row_force + [jnp.zeros((5, chunk), jnp.float32)], 0)
        spread = jnp.concatenate([jnp.where(owner == o, stacked, 0.0) for o in range(owners)], 0)
        a_high, a_low = halves(spread)
        a = jnp.concatenate([a_high, a_low], 0)
        total = total + lax.dot_general(a, tile_hot_ref[:, here], (((1,), (1,)), ((), ())), preferred_element_type=jnp.float32)
    part = total[: owners * 8] + total[owners * 8 :]
    for o in range(owners):
        part_out[o] = part[o * 8 : (o + 1) * 8]


def local(sizes, *args):
    return body(sizes, *args)


def body(sizes, e_field, h_field, current, material, sigma_table, gamma_table, plasma_table, g_kernel,
          surf_cell, surf_owner, surf_tile, surf_normal, row_count):
    n_x, n_y, n_z = sizes
    steps = g_kernel.shape[0]
    planes, rows, lanes = material.shape
    f32 = jnp.float32
    n_msg = 10 * planes
    per_tile = lanes // (2 * steps * planes)
    z_tiles = -(-10 // per_tile)
    n_ghost = 1 if n_y == 2 else 2
    slots = surf_cell.size
    materials = sigma_table.shape[0]
    hbm = pl.BlockSpec(memory_space=pltpu.HBM)

    def shape(*dims, dtype=f32):
        return jax.ShapeDtypeStruct(dims, dtype)

    def grant(mib):
        return pltpu.CompilerParams(vmem_limit_bytes=mib << 20)

    def send(value, axis, second=False):
        return lax.ppermute(value, AXES, full_swap(sizes, axis, second))

    small = [
        sigma_table.reshape(1, materials),
        gamma_table.reshape(1, materials),
        plasma_table.reshape(1, materials),
        g_kernel.reshape(1, steps),
    ] + [v.reshape(1, slots) for v in (surf_cell, surf_owner, surf_tile, surf_normal)]
    args = [v.reshape(3 * planes, rows, lanes) for v in (e_field, h_field, current)] + [material] + small
    packed = pl.pallas_call(
        functools.partial(pack_kernel, steps, n_ghost),
        out_shape=[shape(n_msg, rows, lanes), shape(z_tiles, rows, lanes)]
        + [shape(z_tiles, 8, lanes)] * n_ghost
        + [shape(*v.shape, dtype=v.dtype) for v in small],
        in_specs=[hbm] * len(args),
        out_specs=[VMEM] * (2 + n_ghost + len(small)),
        scratch_shapes=[pltpu.VMEM((planes, rows, lanes), jnp.int32), pltpu.SemaphoreType.DMA((len(args),))],
        compiler_params=grant(4),
        name="pack",
    )(*(pltpu.with_memory_space_constraint(v, pltpu.HBM) for v in args))
    brick, edge, outgoing, small = packed[0], packed[1], packed[2 : 2 + n_ghost], packed[2 + n_ghost :]

    x_first, x_second = send(brick, "gx"), send(brick, "gx", True)
    ghosts = [send(v, "gy", bool(i)) for i, v in enumerate(outgoing)]
    edge = pl.pallas_call(
        functools.partial(widen_kernel, steps, n_y),
        out_shape=shape(z_tiles, rows + 8, lanes),
        in_specs=[VMEM] * (1 + n_ghost),
        out_specs=VMEM,
        compiler_params=grant(2),
        name="widen",
    )(edge, *ghosts)
    edges = pl.pallas_call(
        functools.partial(merge_kernel, steps, n_z),
        out_shape=shape(z_tiles, rows + 8, lanes),
        in_specs=[VMEM] * 2,
        out_specs=VMEM,
        compiler_params=grant(2),
        name="merge",
    )(send(edge, "gz"), send(edge, "gz", True))
    edges = [edges, send(edges, "gx"), send(edges, "gx", True)]

    prepare = pl.pallas_call(
        functools.partial(prepare_kernel, materials, steps, lanes),
        out_shape=[
            shape(4 * materials + steps, 8, lanes),
            shape(lanes, slots, dtype=jnp.bfloat16),
            shape(TILE_DEV, slots, dtype=jnp.bfloat16),
            shape(8, slots, dtype=jnp.int32),
            shape(1, slots),
        ],
        in_specs=[VMEM] * len(small) + [SMEM, pl.BlockSpec(memory_space=pl.ANY)],
        out_specs=[VMEM] * 5,
        compiler_params=grant(6),
        cost_estimate=pl.CostEstimate(flops=1 << 20, bytes_accessed=1 << 20, transcendentals=0),
        name="prepare",
    )
    prepared = prepare(*small, row_count, edges[0])

    bricks = [brick, x_first, x_second]
    outgoing = pl.pallas_call(
        functools.partial(rows_kernel, steps, len(bricks)),
        out_shape=[shape(len(bricks) * n_msg // 2, 8, lanes)] * n_ghost,
        in_specs=[VMEM] * len(bricks) + [pl.BlockSpec(memory_space=pl.ANY)],
        out_specs=[VMEM] * n_ghost,
        compiler_params=grant(6),
        name="rows",
    )(*bricks, prepared[-1])
    ghosts = [send(v, "gy", bool(i)) for i, v in enumerate(outgoing)]

    owners = n_x * n_y
    full = rows + 8
    e_out, h_out, part = pl.pallas_call(
        functools.partial(main_kernel, sizes, steps, materials, n_ghost),
        out_shape=(shape(*e_field.shape), shape(*h_field.shape), shape(owners, 8, TILE_DEV)),
        in_specs=[VMEM] * (len(bricks) + n_ghost + len(edges) + len(prepared)),
        out_specs=(VMEM,) * 3,
        scratch_shapes=[
            pltpu.VMEM((10, 3 * planes, full, lanes), f32),
            pltpu.VMEM((4, 3 * planes, full, lanes), f32),
            pltpu.VMEM((10, full, lanes), f32),
            pltpu.VMEM((4, full, lanes), f32),
            pltpu.VMEM((len(PAIRS), planes * rows, lanes), f32),
        ],
        compiler_params=grant(24),
        name="march",
    )(*bricks, *ghosts, *edges, *prepared)
    got = lax.all_to_all(part, ("gx", "gy"), split_axis=0, concat_axis=0, tiled=True)
    force = jnp.sum(got[:, :3], axis=0)
    return e_out, h_out, force


def solution(mesh):
    sizes = tuple(mesh.shape[a] for a in AXES)
    return jax.shard_map(
        functools.partial(local, sizes),
        mesh=mesh,
        in_specs=(
            P(None, "gx", "gy", "gz"),
            P(None, "gx", "gy", "gz"),
            P(None, "gx", "gy", "gz"),
            P("gx", "gy", "gz"),
            P(),
            P(),
            P(),
            P(),
            P("gx", "gy", "gz", None),
            P("gx", "gy", "gz", None, None),
            P("gx", "gy", "gz", None),
            P("gx", "gy", "gz", None),
            P("gx", "gy", "gz"),
        ),
        out_specs=(
            P(None, "gx", "gy", "gz"),
            P(None, "gx", "gy", "gz"),
            P(None, ("gx", "gy", "gz")),
        ),
        check_vma=False,
    )
```

```python
import functools

import jax
import jax.numpy as jnp
from jax import lax
from jax.experimental import pallas as pl
from jax.experimental.pallas import tpu as pltpu
from jax.sharding import PartitionSpec as P


STEP_DT = 0.5
FACE_AREA = 0.25
TILE_DEV = 128
PAIRS = ((0, 0), (0, 1), (0, 2), (1, 1), (1, 2), (2, 2))
AXES = ("gx", "gy", "gz")
VMEM = pl.BlockSpec(memory_space=pltpu.VMEM)
SMEM = pl.BlockSpec(memory_space=pltpu.SMEM)


def partner(index, size, second):
    if not second:
        return index ^ 1
    return (index - 1) % size if index % 2 == 0 else (index + 1) % size


def full_swap(sizes, axis, second=False):
    pairs = []
    at = AXES.index(axis)
    for x in range(sizes[0]):
        for y in range(sizes[1]):
            for z in range(sizes[2]):
                to = [x, y, z]
                if second and to[at] in (0, sizes[at] - 1) and axis != "gy":
                    to[1] = y ^ 1
                else:
                    to[at] = partner(to[at], sizes[at], second)
                pairs.append(((x * sizes[1] + y) * sizes[2] + z, (to[0] * sizes[1] + to[1]) * sizes[2] + to[2]))
    return pairs


def slot_order(planes):
    end = planes - 1
    head = [(f, 0) for f in (3, 6, 7, 8, 9)]
    tail = [(f, end) for f in (0, 3, 4, 5, 6, 7, 8, 9)]
    rest = [(f, p) for f in range(10) for p in range(planes) if (f, p) not in head + tail]
    return head + rest + tail, len(head), len(head) + len(rest) + len(tail)


def pack_kernel(depth, n_ghost, *refs):
    inputs, refs = refs[:4], refs[4:]
    brick_ref, pay_first, pay_second, edge_ref, refs = *refs[:4], refs[4:]
    sends, bufs, sems = refs[:n_ghost], refs[n_ghost : n_ghost + 4], refs[n_ghost + 4]
    copies = [pltpu.make_async_copy(src, buf, sems.at[i]) for i, (src, buf) in enumerate(zip(inputs, bufs, strict=True))]
    for copy in copies:
        copy.start()
    planes, rows, lanes = bufs[3].shape
    order, _, n_msg = slot_order(planes)
    place = {slot: i for i, slot in enumerate(order)}
    width = 2 * depth * planes
    per_tile = lanes // width
    lane = lax.broadcasted_iota(jnp.int32, (rows, lanes), 1)
    packed = [jnp.zeros((rows, lanes), jnp.float32) for _ in range(edge_ref.shape[0])]
    for f in range(10):
        if f % 3 == 0:
            copies[f // 3].wait()
        for p in range(planes):
            value = (bufs[3][p] + 1).astype(jnp.float32) if f == 9 else bufs[f // 3][f % 3 * planes + p]
            brick_ref[place[f, p]] = value
            tile, start = f // per_tile, f % per_tile * width + p * 2 * depth
            turned = pltpu.roll(value, (start + depth) % lanes, 1)
            packed[tile] = jnp.where((lane >= start) & (lane < start + 2 * depth), turned, packed[tile])
    n_pay = pay_first.shape[0]
    to_upper = n_msg - n_pay
    is_even = lax.axis_index("gx") % 2 == 0
    pay_first[...] = brick_ref[pl.ds(jnp.where(is_even, to_upper, 0), n_pay)]
    pay_second[...] = brick_ref[pl.ds(jnp.where(is_even, 0, to_upper), n_pay)]
    is_odd = lax.axis_index("gy") % 2 == 1
    for tile, value in enumerate(packed):
        edge_ref[tile] = value
        first, last = value[:8], value[rows - 8 :]
        sends[0][tile] = jnp.where(is_odd, first, last)
        if n_ghost > 1:
            sends[1][tile] = jnp.where(is_odd, last, first)


def sides_y(depth, n_y, lanes):
    y = lax.axis_index("gy")
    even = y % 2 == 0
    row = lax.broadcasted_iota(jnp.int32, (8, lanes), 0)
    upper_to = jnp.where(y < n_y - 1, depth, 0)
    lower_from = jnp.where(y > 0, 8 - depth, 8)

    def pick(values):
        if len(values) == 1:
            wanted = (row >= jnp.where(even, 0, lower_from)) & (row < jnp.where(even, upper_to, 8))
            return jnp.where(wanted, values[0], 0.0)
        upper = jnp.where(even, values[0], values[1])
        lower = jnp.where(even, values[1], values[0])
        return jnp.where(row < upper_to, upper, jnp.where(row >= lower_from, lower, 0.0))

    return pick


def widen_kernel(depth, n_y, edge_ref, *refs):
    ghosts, out = refs[:-1], refs[-1]
    pick = sides_y(depth, n_y, edge_ref.shape[2])
    rows = edge_ref.shape[1]
    for tile in range(edge_ref.shape[0]):
        out[tile, :rows] = edge_ref[tile]
        out[tile, rows:] = pick([g[tile] for g in ghosts])


def merge_kernel(depth, n_z, first_ref, second_ref, out_ref):
    z = lax.axis_index("gz")
    even = z % 2 == 0
    shape = out_ref.shape[1:]
    place = lax.broadcasted_iota(jnp.int32, shape, 1) % (2 * depth)
    is_lower = place < jnp.where(z > 0, depth, 0)
    is_upper = place >= jnp.where(z < n_z - 1, depth, 2 * depth)
    for tile in range(out_ref.shape[0]):
        first, second = first_ref[tile], second_ref[tile]
        upper = jnp.where(even, first, second)
        lower = jnp.where(even, second, first)
        out_ref[tile] = jnp.where(is_upper, upper, jnp.where(is_lower, lower, 0.0))


def rows_kernel(depth, n_in, *refs):
    ins, outs = refs[:n_in], refs[n_in + 1 :]
    is_odd = lax.axis_index("gy") % 2
    row = lax.broadcasted_iota(jnp.int32, (8, outs[0].shape[2]), 0)
    planes = [(ref, j) for ref in ins for j in range(ref.shape[0])]
    rows = ins[0].shape[1]
    for which, out in enumerate(outs):
        last = (1 - is_odd) if which == 0 else is_odd
        start = pl.multiple_of(last * (rows - 8), 8)
        mine = (row >= jnp.where(last == 1, 8 - depth, 0)) & (row < jnp.where(last == 1, 8, depth))
        for at in range(0, len(planes), 2):
            value = planes[at][0][planes[at][1], pl.ds(start, 8), :]
            if at + 1 < len(planes):
                turned = planes[at + 1][0][planes[at + 1][1], pl.ds(start, 8), :]
                value = jnp.where(mine, value, pltpu.roll(turned, 4, 0))
            out[at // 2] = value


def prepare_kernel(materials, steps, lanes, *refs):
    inputs, count_ref, refs = refs[:8], refs[8], refs[10:]
    table_ref, hot_ref, tile_hot_ref, ints_ref, scale_ref = refs[:5]
    bufs, sems = refs[5:13], refs[13]
    copies = [pltpu.make_async_copy(src, buf, sems.at[i]) for i, (src, buf) in enumerate(zip(inputs, bufs, strict=True))]
    for copy in copies:
        copy.start()
    for copy in copies:
        copy.wait()
    sigma_ref, gamma_ref, plasma_ref, g_ref, cell_ref, owner_ref, tile_ref, normal_ref = bufs
    slots = cell_ref.shape[1]
    shape = table_ref.shape[1:]

    def splat(ref, at):
        return jnp.broadcast_to(ref[:, at : at + 1], shape)

    for which in range(materials):
        sigma, gamma, plasma = splat(sigma_ref, which), splat(gamma_ref, which), splat(plasma_ref, which)
        table_ref[4 * which] = (1.0 - sigma * STEP_DT / 2) / (1.0 + sigma * STEP_DT / 2)
        table_ref[4 * which + 1] = STEP_DT / (1.0 + sigma * STEP_DT / 2)
        table_ref[4 * which + 2] = (1.0 - gamma * STEP_DT / 2) / (1.0 + gamma * STEP_DT / 2)
        table_ref[4 * which + 3] = plasma * STEP_DT / (1.0 + gamma * STEP_DT / 2)
    for t in range(steps):
        table_ref[4 * materials + t] = splat(g_ref, t)
    cell, normal = cell_ref[...], normal_ref[...]
    in_lane, in_row = cell % lanes, cell // lanes
    hot = lax.broadcasted_iota(jnp.int32, (lanes, slots), 0) == in_lane
    hot_ref[...] = jnp.where(hot, 1.0, 0.0).astype(jnp.bfloat16)
    tile_hot = lax.broadcasted_iota(jnp.int32, (TILE_DEV, slots), 0) == tile_ref[...]
    tile_hot_ref[...] = jnp.where(tile_hot, 1.0, 0.0).astype(jnp.bfloat16)
    ints_ref[0:1] = in_row
    ints_ref[1:2] = owner_ref[...]
    ints_ref[2:3] = normal // 2
    live = lax.broadcasted_iota(jnp.int32, (1, slots), 1) < count_ref[0, 0, 0]
    sign = (1 - 2 * (normal % 2)).astype(jnp.float32)
    scale_ref[...] = jnp.where(live, FACE_AREA * sign, 0.0)


def main_kernel(sizes, steps, materials, n_ghost, *refs):
    n_x, n_y, _ = sizes
    bricks, ghosts, refs = refs[:3], refs[3 : 3 + n_ghost], refs[3 + n_ghost :]
    edge_refs, refs = refs[:3], refs[3:]
    table_ref, hot_ref, tile_hot_ref, ints_ref, scale_ref = refs[:5]
    e_out, h_out, part_out = refs[5:8]
    field, coef, side, side_coef, tensor, sems = refs[8:14]
    n_msg, rows, lanes = bricks[0].shape
    planes = e_out.shape[1]
    depth = steps
    x, y, z = (lax.axis_index(a) for a in AXES)
    even_x = x % 2 == 0
    low_x, high_x, low_y, low_z = x > 0, x < n_x - 1, y > 0, z > 0
    pick = sides_y(depth, n_y, lanes)
    full = rows + 8

    order, _, _ = slot_order(planes)
    place = {slot: i for i, slot in enumerate(order)}
    n_pay = bricks[1].shape[0]

    def whole(which, j):
        at = j if which == 0 else n_msg + (which - 1) * n_pay + j
        values = [g[at // 2] for g in ghosts]
        if at % 2:
            values = [pltpu.roll(v, 4, 0) for v in values]
        return jnp.concatenate([bricks[which][j], pick(values)], 0)

    for f, p in order:
        field[f, planes + p] = whole(0, place[f, p])
        at = place[f, p] - (n_msg - n_pay)
        if at >= 0:
            first, second = whole(1, at), whole(2, at)
            field[f, p] = jnp.where(low_x, jnp.where(even_x, second, first), 0.0)
        at = place[f, p]
        if at < n_pay:
            first, second = whole(1, at), whole(2, at)
            field[f, 2 * planes + p] = jnp.where(high_x, jnp.where(even_x, first, second), 0.0)

    width = 2 * depth * planes
    per_tile = lanes // width
    lane = lax.broadcasted_iota(jnp.int32, (full, lanes), 1)
    at_low = lane < jnp.where(low_x, width, 0)
    at_own = (lane >= width) & (lane < 2 * width)
    at_high = (lane >= 2 * width) & (lane < jnp.where(high_x, 3 * width, 0))
    tiles = []
    for tile in range(edge_refs[0].shape[0]):
        own, first, second = (r[tile] for r in edge_refs)
        tiles.append((jnp.where(even_x, second, first), own, jnp.where(even_x, first, second)))
    for f in range(n_msg // planes):
        start = f % per_tile * width
        low, own, high = (
            pltpu.roll(v, (cls * width - start) % lanes, 1) if cls * width != start else v
            for cls, v in enumerate(tiles[f // per_tile])
        )
        side[f] = jnp.where(at_low, low, jnp.where(at_own, own, jnp.where(at_high, high, 0.0)))

    table = [[table_ref[4 * m + i] for i in range(4)] for m in range(materials)]

    def look_up(code, which):
        value = jnp.zeros((8, lanes), jnp.float32)
        for m in range(materials):
            value = jnp.where(code == float(m + 1), table[m][which], value)
        return value

    for r in range(0, full, 8):
        for which in range(4):
            for plane in range(1, 3 * planes - 1):
                coef[which, plane, r : r + 8] = look_up(field[9, plane, r : r + 8], which)
            side_coef[which, r : r + 8] = look_up(side[9, r : r + 8], which)

    row = lax.broadcasted_iota(jnp.int32, (full, lanes), 0)
    dt_all = jnp.where(row < jnp.where(low_y, full, full - depth), STEP_DT, 0.0)
    dt_low = jnp.where(low_x, dt_all, 0.0)
    dt_side = jnp.where((lane >= jnp.where(low_x, 0, width)) & (lane < 3 * width), dt_all, 0.0)
    dt_side = jnp.where(lane % (2 * depth) >= jnp.where(low_z, 0, depth), dt_side, 0.0)

    def turn(v, by):
        by = by % lanes
        return pltpu.roll(v, by, 1) if by else v

    def next_y(v):
        return pltpu.roll(v, full - 1, 0)

    def prev_y(v):
        return pltpu.roll(v, 1, 0)

    def above(plane):
        return 2 * depth * plane + depth

    def next_z(v, ghost, plane):
        return jnp.where(lane == lanes - 1, turn(ghost, lanes - 1 - above(plane)), turn(v, -1))

    def prev_z(v, ghost, plane):
        return jnp.where(lane == 0, turn(ghost, 1 - above(plane)), turn(v, 1))

    last = 3 * planes - 1
    for t in range(1, steps + 1):
        final = t == steps
        keep_rows = rows if final else full
        h_planes = range(t - 1, last - t + 1)
        ex, ey, ez, hx, hy, hz = (side[i] for i in range(6))
        ex_z, ey_z = turn(ex, -1), turn(ey, -1)
        for plane in h_planes:
            here = lane == above(plane) - 1
            ex_z = jnp.where(here, turn(field[0, plane], above(plane) - 1), ex_z)
            ey_z = jnp.where(here, turn(field[1, plane], above(plane) - 1), ey_z)
        ey_x, ez_x = turn(ey, -2 * depth), turn(ez, -2 * depth)
        ghx = hx - dt_side * ((next_y(ez) - ez) - (ey_z - ey))
        ghy = hy - dt_side * ((ex_z - ex) - (ez_x - ez))
        ghz = hz - dt_side * ((ey_x - ey) - (next_y(ex) - ex))
        gex, gey, gez = ex, ey, ez
        hx_above, hy_above = turn(ghx, 1), turn(ghy, 1)
        for plane in h_planes:
            ex, ey, ez = field[0, plane], field[1, plane], field[2, plane]
            hx, hy, hz = field[3, plane], field[4, plane], field[5, plane]
            ey_x, ez_x = field[1, plane + 1], field[2, plane + 1]
            dt = dt_low if plane < planes else dt_all
            hy = hy - dt * ((next_z(ex, gex, plane) - ex) - (ez_x - ez))
            hz = hz - dt * ((ey_x - ey) - (next_y(ex) - ex))
            field[4, plane] = hy
            field[5, plane] = hz
            if plane < t:
                continue
            hx = hx - dt * ((next_y(ez) - ez) - (next_z(ey, gey, plane) - ey))
            field[3, plane] = hx
            if not final:
                here = lane == above(plane)
                hx_above = jnp.where(here, turn(hx, above(plane) - (lanes - 1)), hx_above)
                hy_above = jnp.where(here, turn(hy, above(plane) - (lanes - 1)), hy_above)
            hy_x, hz_x = field[4, plane - 1], field[5, plane - 1]
            curls = (
                (hz - prev_y(hz)) - (hy - prev_z(hy, ghy, plane)),
                (hx - prev_z(hx, ghx, plane)) - (hz - hz_x),
                (hy - hy_x) - (hx - prev_y(hx)),
            )
            keep_e, gain_e, keep_j, gain_j = (coef[i, plane, :keep_rows] for i in range(4))
            for comp, (old, curl) in enumerate(zip((ex, ey, ez), curls, strict=True)):
                drude = keep_j * field[6 + comp, plane, :keep_rows] + gain_j * old[:keep_rows]
                if not final:
                    field[6 + comp, plane] = drude
                field[comp, plane, :keep_rows] = keep_e * old[:keep_rows] + gain_e * (curl[:keep_rows] - drude)
        if not final:
            side[3], side[4], side[5] = ghx, ghy, ghz
            hy_x, hz_x = turn(ghy, 2 * depth), turn(ghz, 2 * depth)
            curls = (
                (ghz - prev_y(ghz)) - (ghy - hy_above),
                (ghx - hx_above) - (ghz - hz_x),
                (ghy - hy_x) - (ghx - prev_y(ghx)),
            )
            keep_e, gain_e, keep_j, gain_j = (side_coef[i] for i in range(4))
            for comp, (old, curl) in enumerate(zip((gex, gey, gez), curls, strict=True)):
                drude = keep_j * side[6 + comp] + gain_j * old
                side[6 + comp] = drude
                side[comp] = keep_e * old + gain_e * (curl - drude)
        g = table_ref[4 * materials + t - 1]
        g = jnp.concatenate([g] * (rows // 8), 0)
        for plane in range(planes):
            e = [field[i, planes + plane, :rows] for i in range(3)]
            h = [field[3 + i, planes + plane, :rows] for i in range(3)]
            prod = {p: e[p[0]] * e[p[1]] + h[p[0]] * h[p[1]] for p in PAIRS}
            energy = 0.5 * (prod[0, 0] + prod[1, 1] + prod[2, 2])
            for i, p in enumerate(PAIRS):
                value = prod[p] - energy if p[0] == p[1] else prod[p]
                value = g * value
                if t > 1:
                    value = tensor[i, pl.ds(plane * rows, rows), :] + value
                tensor[i, pl.ds(plane * rows, rows), :] = value
        if final:
            own = pl.ds(planes, planes)
            outs = [
                pltpu.make_async_copy(field.at[pl.ds(3 * i, 3), own, pl.ds(0, rows)], out, sems.at[i])
                for i, out in enumerate((e_out, h_out))
            ]
            for copy in outs:
                copy.start()

    def halves(v):
        high = v.astype(jnp.bfloat16)
        return high, (v - high.astype(jnp.float32)).astype(jnp.bfloat16)

    cells = planes * rows
    high, low = halves(tensor[...].reshape(len(PAIRS) * cells, lanes))
    lhs = jnp.concatenate([high, low], 1)
    slots = hot_ref.shape[1]
    owners = part_out.shape[0]
    chunk = 256
    total = jnp.zeros((2 * owners * 8, TILE_DEV), jnp.float32)
    for at in range(0, slots, chunk):
        here = slice(at, at + chunk)
        in_row, owner, axis = ints_ref[0:1, here], ints_ref[1:2, here], ints_ref[2:3, here]
        hot = hot_ref[:, here]
        picked = jnp.dot(lhs, jnp.concatenate([hot, hot], 0), preferred_element_type=jnp.float32)
        in_row = lax.broadcasted_iota(jnp.int32, (cells, chunk), 0) == in_row
        vals = {
            p: jnp.sum(jnp.where(in_row, picked[i * cells : (i + 1) * cells], 0.0), axis=0, keepdims=True)
            for i, p in enumerate(PAIRS)
        }
        row_force = []
        for i in range(3):
            by = [vals[min(i, a), max(i, a)] for a in range(3)]
            row_force.append(scale_ref[:, here] * jnp.where(axis == 0, by[0], jnp.where(axis == 1, by[1], by[2])))
        stacked = jnp.concatenate(row_force + [jnp.zeros((5, chunk), jnp.float32)], 0)
        spread = jnp.concatenate([jnp.where(owner == o, stacked, 0.0) for o in range(owners)], 0)
        a_high, a_low = halves(spread)
        a = jnp.concatenate([a_high, a_low], 0)
        total = total + lax.dot_general(a, tile_hot_ref[:, here], (((1,), (1,)), ((), ())), preferred_element_type=jnp.float32)
    part = total[: owners * 8] + total[owners * 8 :]
    for o in range(owners):
        part_out[o] = part[o * 8 : (o + 1) * 8]
    for copy in outs:
        copy.wait()


def local(sizes, *args):
    return body(sizes, *args)


def body(sizes, e_field, h_field, current, material, sigma_table, gamma_table, plasma_table, g_kernel,
          surf_cell, surf_owner, surf_tile, surf_normal, row_count):
    n_x, n_y, n_z = sizes
    steps = g_kernel.shape[0]
    planes, rows, lanes = material.shape
    f32 = jnp.float32
    _, head, n_msg = slot_order(planes)
    n_pay = n_msg - head
    per_tile = lanes // (2 * steps * planes)
    z_tiles = -(-10 // per_tile)
    n_ghost = 1 if n_y == 2 else 2
    slots = surf_cell.size
    materials = sigma_table.shape[0]
    hbm = pl.BlockSpec(memory_space=pltpu.HBM)

    def shape(*dims, dtype=f32):
        return jax.ShapeDtypeStruct(dims, dtype)

    def grant(mib):
        return pltpu.CompilerParams(vmem_limit_bytes=mib << 20)

    def send(value, axis, second=False):
        return lax.ppermute(value, AXES, full_swap(sizes, axis, second))

    small = [
        sigma_table.reshape(1, materials),
        gamma_table.reshape(1, materials),
        plasma_table.reshape(1, materials),
        g_kernel.reshape(1, steps),
    ] + [v.reshape(1, slots) for v in (surf_cell, surf_owner, surf_tile, surf_normal)]
    small = [pltpu.with_memory_space_constraint(v, pltpu.HBM) for v in small]
    args = [v.reshape(3 * planes, rows, lanes) for v in (e_field, h_field, current)] + [material]
    packed = pl.pallas_call(
        functools.partial(pack_kernel, steps, n_ghost),
        out_shape=[shape(n_msg, rows, lanes), shape(n_pay, rows, lanes), shape(n_pay, rows, lanes), shape(z_tiles, rows, lanes)]
        + [shape(z_tiles, 8, lanes)] * n_ghost,
        in_specs=[hbm] * len(args),
        out_specs=[VMEM] * (4 + n_ghost),
        scratch_shapes=[pltpu.VMEM(v.shape, v.dtype) for v in args] + [pltpu.SemaphoreType.DMA((len(args),))],
        compiler_params=grant(4),
        name="pack",
    )(*(pltpu.with_memory_space_constraint(v, pltpu.HBM) for v in args))
    brick, pay_first, pay_second, edge = packed[:4]
    outgoing = packed[4:]

    x_first, x_second = send(pay_first, "gx"), send(pay_second, "gx", True)
    ghosts = [send(v, "gy", bool(i)) for i, v in enumerate(outgoing)]
    edge = pl.pallas_call(
        functools.partial(widen_kernel, steps, n_y),
        out_shape=shape(z_tiles, rows + 8, lanes),
        in_specs=[VMEM] * (1 + n_ghost),
        out_specs=VMEM,
        compiler_params=grant(2),
        name="widen",
    )(edge, *ghosts)
    edges = pl.pallas_call(
        functools.partial(merge_kernel, steps, n_z),
        out_shape=shape(z_tiles, rows + 8, lanes),
        in_specs=[VMEM] * 2,
        out_specs=VMEM,
        compiler_params=grant(2),
        name="merge",
    )(send(edge, "gz"), send(edge, "gz", True))
    edges = [edges, send(edges, "gx"), send(edges, "gx", True)]

    prepare = pl.pallas_call(
        functools.partial(prepare_kernel, materials, steps, lanes),
        out_shape=[
            shape(4 * materials + steps, 8, lanes),
            shape(lanes, slots, dtype=jnp.bfloat16),
            shape(TILE_DEV, slots, dtype=jnp.bfloat16),
            shape(8, slots, dtype=jnp.int32),
            shape(1, slots),
        ],
        in_specs=[hbm] * len(small) + [SMEM, pl.BlockSpec(memory_space=pl.ANY)],
        out_specs=[VMEM] * 5,
        scratch_shapes=[pltpu.VMEM(v.shape, v.dtype) for v in small] + [pltpu.SemaphoreType.DMA((len(small),))],
        compiler_params=grant(6),
        cost_estimate=pl.CostEstimate(flops=1 << 20, bytes_accessed=1 << 20, transcendentals=0),
        name="prepare",
    )
    prepared = prepare(*small, row_count, edges[0])

    bricks = [brick, x_first, x_second]
    outgoing = pl.pallas_call(
        functools.partial(rows_kernel, steps, len(bricks)),
        out_shape=[shape(-(-(n_msg + 2 * n_pay) // 2), 8, lanes)] * n_ghost,
        in_specs=[VMEM] * len(bricks) + [pl.BlockSpec(memory_space=pl.ANY)],
        out_specs=[VMEM] * n_ghost,
        compiler_params=grant(6),
        name="rows",
    )(*bricks, prepared[-1])
    ghosts = [send(v, "gy", bool(i)) for i, v in enumerate(outgoing)]

    owners = n_x * n_y
    full = rows + 8
    e_out, h_out, part = pl.pallas_call(
        functools.partial(main_kernel, sizes, steps, materials, n_ghost),
        out_shape=(shape(*e_field.shape), shape(*h_field.shape), shape(owners, 8, TILE_DEV)),
        in_specs=[VMEM] * (len(bricks) + n_ghost + len(edges) + len(prepared)),
        out_specs=(hbm, hbm, VMEM),
        scratch_shapes=[
            pltpu.VMEM((10, 3 * planes, full, lanes), f32),
            pltpu.VMEM((4, 3 * planes, full, lanes), f32),
            pltpu.VMEM((10, full, lanes), f32),
            pltpu.VMEM((4, full, lanes), f32),
            pltpu.VMEM((len(PAIRS), planes * rows, lanes), f32),
            pltpu.SemaphoreType.DMA((2,)),
        ],
        compiler_params=grant(24),
        name="march",
    )(*bricks, *ghosts, *edges, *prepared)
    got = lax.all_to_all(part, ("gx", "gy"), split_axis=0, concat_axis=0, tiled=True)
    force = jnp.sum(got[:, :3], axis=0)
    return e_out, h_out, force


def solution(mesh):
    sizes = tuple(mesh.shape[a] for a in AXES)
    return jax.shard_map(
        functools.partial(local, sizes),
        mesh=mesh,
        in_specs=(
            P(None, "gx", "gy", "gz"),
            P(None, "gx", "gy", "gz"),
            P(None, "gx", "gy", "gz"),
            P("gx", "gy", "gz"),
            P(),
            P(),
            P(),
            P(),
            P("gx", "gy", "gz", None),
            P("gx", "gy", "gz", None, None),
            P("gx", "gy", "gz", None),
            P("gx", "gy", "gz", None),
            P("gx", "gy", "gz"),
        ),
        out_specs=(
            P(None, "gx", "gy", "gz"),
            P(None, "gx", "gy", "gz"),
            P(None, ("gx", "gy", "gz")),
        ),
        check_vma=False,
    )
```

```python
import functools

import jax
import jax.numpy as jnp
from jax import lax
from jax.experimental import pallas as pl
from jax.experimental.pallas import tpu as pltpu
from jax.sharding import PartitionSpec as P


STEP_DT = 0.5
FACE_AREA = 0.25
TILE_DEV = 128
PAIRS = ((0, 0), (0, 1), (0, 2), (1, 1), (1, 2), (2, 2))
AXES = ("gx", "gy", "gz")
VMEM = pl.BlockSpec(memory_space=pltpu.VMEM)
SMEM = pl.BlockSpec(memory_space=pltpu.SMEM)


def partner(index, size, second):
    if not second:
        return index ^ 1
    return (index - 1) % size if index % 2 == 0 else (index + 1) % size


def full_swap(sizes, axis, second=False):
    pairs = []
    at = AXES.index(axis)
    for x in range(sizes[0]):
        for y in range(sizes[1]):
            for z in range(sizes[2]):
                to = [x, y, z]
                if second and to[at] in (0, sizes[at] - 1) and axis != "gy":
                    to[1] = y ^ 1
                else:
                    to[at] = partner(to[at], sizes[at], second)
                pairs.append(((x * sizes[1] + y) * sizes[2] + z, (to[0] * sizes[1] + to[1]) * sizes[2] + to[2]))
    return pairs


def slot_order(planes):
    end = planes - 1
    head = [(f, 0) for f in (3, 6, 7, 8, 9)]
    tail = [(f, end) for f in (0, 3, 4, 5, 6, 7, 8, 9)]
    rest = [(f, p) for f in range(10) for p in range(planes) if (f, p) not in head + tail]
    return head + rest + tail, len(head), len(head) + len(rest) + len(tail)


def pack_kernel(depth, n_ghost, *refs):
    inputs, refs = refs[:4], refs[4:]
    brick_ref, pay_first, pay_second, edge_ref, refs = *refs[:4], refs[4:]
    sends, bufs, sems = refs[:n_ghost], refs[n_ghost : n_ghost + 4], refs[n_ghost + 4]
    copies = [pltpu.make_async_copy(src, buf, sems.at[i]) for i, (src, buf) in enumerate(zip(inputs, bufs, strict=True))]
    for copy in copies:
        copy.start()
    planes, rows, lanes = bufs[3].shape
    order, _, n_msg = slot_order(planes)
    place = {slot: i for i, slot in enumerate(order)}
    width = 2 * depth * planes
    per_tile = lanes // width
    lane = lax.broadcasted_iota(jnp.int32, (rows, lanes), 1)
    packed = [jnp.zeros((rows, lanes), jnp.float32) for _ in range(edge_ref.shape[0])]
    for f in range(10):
        if f % 3 == 0:
            copies[f // 3].wait()
        for p in range(planes):
            value = (bufs[3][p] + 1).astype(jnp.float32) if f == 9 else bufs[f // 3][f % 3 * planes + p]
            brick_ref[place[f, p]] = value
            tile, start = f // per_tile, f % per_tile * width + p * 2 * depth
            turned = pltpu.roll(value, (start + depth) % lanes, 1)
            packed[tile] = jnp.where((lane >= start) & (lane < start + 2 * depth), turned, packed[tile])
    n_pay = pay_first.shape[0]
    to_upper = n_msg - n_pay
    is_even = lax.axis_index("gx") % 2 == 0
    pay_first[...] = brick_ref[pl.ds(jnp.where(is_even, to_upper, 0), n_pay)]
    pay_second[...] = brick_ref[pl.ds(jnp.where(is_even, 0, to_upper), n_pay)]
    is_odd = lax.axis_index("gy") % 2 == 1
    for tile, value in enumerate(packed):
        edge_ref[tile] = value
        first, last = value[:8], value[rows - 8 :]
        sends[0][tile] = jnp.where(is_odd, first, last)
        if n_ghost > 1:
            sends[1][tile] = jnp.where(is_odd, last, first)


def sides_y(depth, n_y, lanes):
    y = lax.axis_index("gy")
    even = y % 2 == 0
    row = lax.broadcasted_iota(jnp.int32, (8, lanes), 0)
    upper_to = jnp.where(y < n_y - 1, depth, 0)
    lower_from = jnp.where(y > 0, 8 - depth, 8)

    def pick(values):
        if len(values) == 1:
            wanted = (row >= jnp.where(even, 0, lower_from)) & (row < jnp.where(even, upper_to, 8))
            return jnp.where(wanted, values[0], 0.0)
        upper = jnp.where(even, values[0], values[1])
        lower = jnp.where(even, values[1], values[0])
        return jnp.where(row < upper_to, upper, jnp.where(row >= lower_from, lower, 0.0))

    return pick


def widen_kernel(depth, n_y, edge_ref, *refs):
    ghosts, out = refs[:-1], refs[-1]
    pick = sides_y(depth, n_y, edge_ref.shape[2])
    rows = edge_ref.shape[1]
    for tile in range(edge_ref.shape[0]):
        out[tile, :rows] = edge_ref[tile]
        out[tile, rows:] = pick([g[tile] for g in ghosts])


def merge_kernel(depth, n_z, count_ref, first_ref, second_ref, out_ref, count_out):
    count_out[...] = jnp.full(count_out.shape, count_ref[0, 0, 0], jnp.int32)
    z = lax.axis_index("gz")
    even = z % 2 == 0
    shape = out_ref.shape[1:]
    place = lax.broadcasted_iota(jnp.int32, shape, 1) % (2 * depth)
    is_lower = place < jnp.where(z > 0, depth, 0)
    is_upper = place >= jnp.where(z < n_z - 1, depth, 2 * depth)
    for tile in range(out_ref.shape[0]):
        first, second = first_ref[tile], second_ref[tile]
        upper = jnp.where(even, first, second)
        lower = jnp.where(even, second, first)
        out_ref[tile] = jnp.where(is_upper, upper, jnp.where(is_lower, lower, 0.0))


def rows_kernel(depth, n_in, *refs):
    ins, outs = refs[:n_in], refs[n_in:]
    is_odd = lax.axis_index("gy") % 2
    row = lax.broadcasted_iota(jnp.int32, (8, outs[0].shape[2]), 0)
    planes = [(ref, j) for ref in ins for j in range(ref.shape[0])]
    rows = ins[0].shape[1]
    for which, out in enumerate(outs):
        last = (1 - is_odd) if which == 0 else is_odd
        start = pl.multiple_of(last * (rows - 8), 8)
        mine = (row >= jnp.where(last == 1, 8 - depth, 0)) & (row < jnp.where(last == 1, 8, depth))
        for at in range(0, len(planes), 2):
            value = planes[at][0][planes[at][1], pl.ds(start, 8), :]
            if at + 1 < len(planes):
                turned = planes[at + 1][0][planes[at + 1][1], pl.ds(start, 8), :]
                value = jnp.where(mine, value, pltpu.roll(turned, 4, 0))
            out[at // 2] = value


def look_up(table, code, which):
    value = jnp.zeros(code.shape, jnp.float32)
    for m, row in enumerate(table):
        value = jnp.where(code == float(m + 1), row[which], value)
    return value


def prepare_kernel(n_x, n_y, paired, materials, steps, lanes, *refs):
    inputs, count_ref, bricks, refs = refs[:8], refs[8], refs[9:12], refs[12:]
    table_ref, hot_ref, tile_hot_ref, ints_ref, scale_ref, beside_ref, coef_ref = refs[:7]
    bufs, sems = refs[7:15], refs[15]
    copies = [pltpu.make_async_copy(src, buf, sems.at[i]) for i, (src, buf) in enumerate(zip(inputs, bufs, strict=True))]
    for copy in copies:
        copy.start()
    planes = beside_ref.shape[1] // 2
    order, _, n_msg = slot_order(planes)
    place = {slot: i for i, slot in enumerate(order)}
    n_pay = bricks[1].shape[0]
    x = lax.axis_index("gx")
    even = x % 2 == 0
    codes = {}
    for f, p in order:
        for upper in (False, True):
            at = place[f, p] - (0 if upper else n_msg - n_pay)
            if not 0 <= at < n_pay:
                continue
            first, second = bricks[1][at], bricks[2][at]
            value = jnp.where(even, first, second) if upper else jnp.where(even, second, first)
            value = jnp.where(x < n_x - 1 if upper else x > 0, value, 0.0)
            if f == 9:
                codes[(2 * planes if upper else 0) + p] = value
            else:
                beside_ref[f, (planes if upper else 0) + p] = value
    for p in range(planes):
        codes[planes + p] = bricks[0][place[9, p]]
    for copy in copies:
        copy.wait()
    sigma_ref, gamma_ref, plasma_ref, g_ref, cell_ref, owner_ref, tile_ref, normal_ref = bufs
    slots = cell_ref.shape[1]
    shape = table_ref.shape[1:]

    def splat(ref, at):
        return jnp.broadcast_to(ref[:, at : at + 1], shape)

    for which in range(materials):
        sigma, gamma, plasma = splat(sigma_ref, which), splat(gamma_ref, which), splat(plasma_ref, which)
        table_ref[4 * which] = (1.0 - sigma * STEP_DT / 2) / (1.0 + sigma * STEP_DT / 2)
        table_ref[4 * which + 1] = STEP_DT / (1.0 + sigma * STEP_DT / 2)
        table_ref[4 * which + 2] = (1.0 - gamma * STEP_DT / 2) / (1.0 + gamma * STEP_DT / 2)
        table_ref[4 * which + 3] = plasma * STEP_DT / (1.0 + gamma * STEP_DT / 2)
    for t in range(steps):
        table_ref[4 * materials + t] = splat(g_ref, t)
    table = [[table_ref[4 * m + i] for i in range(4)] for m in range(materials)]
    for plane, code in codes.items():
        for r in range(0, code.shape[0], 8):
            for which in range(4):
                coef_ref[which, plane, r : r + 8] = look_up(table, code[r : r + 8], which)
    cell, normal = cell_ref[...], normal_ref[...]
    in_lane, in_row = cell % lanes, cell // lanes
    hot = lax.broadcasted_iota(jnp.int32, (lanes, slots), 0) == in_lane
    hot_ref[...] = jnp.where(hot, 1.0, 0.0).astype(jnp.bfloat16)
    tile_hot = lax.broadcasted_iota(jnp.int32, (TILE_DEV, slots), 0) == tile_ref[...]
    tile_hot_ref[...] = jnp.where(tile_hot, 1.0, 0.0).astype(jnp.bfloat16)
    ints_ref[0:1] = in_row
    self_index = x * n_y + lax.axis_index("gy") if paired else 0
    ints_ref[1:2] = jnp.bitwise_xor(owner_ref[...], self_index)
    ints_ref[2:3] = normal // 2
    live = lax.broadcasted_iota(jnp.int32, (1, slots), 1) < count_ref[:, :1]
    sign = (1 - 2 * (normal % 2)).astype(jnp.float32)
    scale_ref[...] = jnp.where(live, FACE_AREA * sign, 0.0)


def main_kernel(sizes, steps, materials, n_ghost, n_part, *refs):
    n_x, n_y, _ = sizes
    bricks, ghosts, refs = refs[:3], refs[3 : 3 + n_ghost], refs[3 + n_ghost :]
    edge_refs, refs = refs[:3], refs[3:]
    table_ref, hot_ref, tile_hot_ref, ints_ref, scale_ref, beside_ref, coef_ref = refs[:7]
    e_out, h_out, refs = refs[7], refs[8], refs[9:]
    part_outs, refs = refs[:n_part], refs[n_part:]
    field, coef, side, side_coef, tensor, sems = refs
    n_msg, rows, lanes = bricks[0].shape
    planes = e_out.shape[1]
    depth = steps
    x, y, z = (lax.axis_index(a) for a in AXES)
    even_x = x % 2 == 0
    low_x, high_x, low_y, low_z = x > 0, x < n_x - 1, y > 0, z > 0
    pick = sides_y(depth, n_y, lanes)
    full = rows + 8

    order, _, _ = slot_order(planes)
    place = {slot: i for i, slot in enumerate(order)}
    n_pay = bricks[1].shape[0]

    def tile_of(which, j):
        at = j if which == 0 else n_msg + (which - 1) * n_pay + j
        values = [g[at // 2] for g in ghosts]
        if at % 2:
            values = [pltpu.roll(v, 4, 0) for v in values]
        return pick(values)

    codes = {}

    def put(f, plane, main, tile):
        if f == 9:
            codes[plane] = tile
        else:
            field[f, plane, :rows] = main
            field[f, plane, rows:] = tile

    for f, p in order:
        put(f, planes + p, None if f == 9 else bricks[0][place[f, p]], tile_of(0, place[f, p]))
        at = place[f, p] - (n_msg - n_pay)
        if at >= 0:
            first, second = tile_of(1, at), tile_of(2, at)
            put(f, p, None if f == 9 else beside_ref[f, p], jnp.where(low_x, jnp.where(even_x, second, first), 0.0))
        at = place[f, p]
        if at < n_pay:
            first, second = tile_of(1, at), tile_of(2, at)
            put(f, 2 * planes + p, None if f == 9 else beside_ref[f, planes + p], jnp.where(high_x, jnp.where(even_x, first, second), 0.0))

    width = 2 * depth * planes
    per_tile = lanes // width
    lane = lax.broadcasted_iota(jnp.int32, (full, lanes), 1)
    at_low = lane < jnp.where(low_x, width, 0)
    at_own = (lane >= width) & (lane < 2 * width)
    at_high = (lane >= 2 * width) & (lane < jnp.where(high_x, 3 * width, 0))
    tiles = []
    for tile in range(edge_refs[0].shape[0]):
        own, first, second = (r[tile] for r in edge_refs)
        tiles.append((jnp.where(even_x, second, first), own, jnp.where(even_x, first, second)))
    for f in range(n_msg // planes):
        start = f % per_tile * width
        low, own, high = (
            pltpu.roll(v, (cls * width - start) % lanes, 1) if cls * width != start else v
            for cls, v in enumerate(tiles[f // per_tile])
        )
        side[f] = jnp.where(at_low, low, jnp.where(at_own, own, jnp.where(at_high, high, 0.0)))

    table = [[table_ref[4 * m + i] for i in range(4)] for m in range(materials)]

    for which in range(4):
        for plane in range(1, 3 * planes - 1):
            coef[which, plane] = look_up(table, codes[plane], which)
        for r in range(0, full, 8):
            side_coef[which, r : r + 8] = look_up(table, side[9, r : r + 8], which)

    row = lax.broadcasted_iota(jnp.int32, (full, lanes), 0)
    dt_all = jnp.where(row < jnp.where(low_y, full, full - depth), STEP_DT, 0.0)
    dt_low = jnp.where(low_x, dt_all, 0.0)
    dt_side = jnp.where((lane >= jnp.where(low_x, 0, width)) & (lane < 3 * width), dt_all, 0.0)
    dt_side = jnp.where(lane % (2 * depth) >= jnp.where(low_z, 0, depth), dt_side, 0.0)

    def turn(v, by):
        by = by % lanes
        return pltpu.roll(v, by, 1) if by else v

    def next_y(v):
        return pltpu.roll(v, full - 1, 0)

    def prev_y(v):
        return pltpu.roll(v, 1, 0)

    def above(plane):
        return 2 * depth * plane + depth

    def next_z(v, ghost, plane):
        return jnp.where(lane == lanes - 1, turn(ghost, lanes - 1 - above(plane)), turn(v, -1))

    def prev_z(v, ghost, plane):
        return jnp.where(lane == 0, turn(ghost, 1 - above(plane)), turn(v, 1))

    last = 3 * planes - 1
    for t in range(1, steps + 1):
        final = t == steps
        keep_rows = rows if final else full
        h_planes = range(t - 1, last - t + 1)
        ex, ey, ez, hx, hy, hz = (side[i] for i in range(6))
        ex_z, ey_z = turn(ex, -1), turn(ey, -1)
        for plane in h_planes:
            here = lane == above(plane) - 1
            ex_z = jnp.where(here, turn(field[0, plane], above(plane) - 1), ex_z)
            ey_z = jnp.where(here, turn(field[1, plane], above(plane) - 1), ey_z)
        ey_x, ez_x = turn(ey, -2 * depth), turn(ez, -2 * depth)
        ghx = hx - dt_side * ((next_y(ez) - ez) - (ey_z - ey))
        ghy = hy - dt_side * ((ex_z - ex) - (ez_x - ez))
        ghz = hz - dt_side * ((ey_x - ey) - (next_y(ex) - ex))
        gex, gey, gez = ex, ey, ez
        hx_above, hy_above = turn(ghx, 1), turn(ghy, 1)
        for plane in h_planes:
            ex, ey, ez = field[0, plane], field[1, plane], field[2, plane]
            hx, hy, hz = field[3, plane], field[4, plane], field[5, plane]
            ey_x, ez_x = field[1, plane + 1], field[2, plane + 1]
            dt = dt_low if plane < planes else dt_all
            hy = hy - dt * ((next_z(ex, gex, plane) - ex) - (ez_x - ez))
            hz = hz - dt * ((ey_x - ey) - (next_y(ex) - ex))
            field[4, plane] = hy
            field[5, plane] = hz
            if plane < t:
                continue
            hx = hx - dt * ((next_y(ez) - ez) - (next_z(ey, gey, plane) - ey))
            field[3, plane] = hx
            if not final:
                here = lane == above(plane)
                hx_above = jnp.where(here, turn(hx, above(plane) - (lanes - 1)), hx_above)
                hy_above = jnp.where(here, turn(hy, above(plane) - (lanes - 1)), hy_above)
            hy_x, hz_x = field[4, plane - 1], field[5, plane - 1]
            curls = (
                (hz - prev_y(hz)) - (hy - prev_z(hy, ghy, plane)),
                (hx - prev_z(hx, ghx, plane)) - (hz - hz_x),
                (hy - hy_x) - (hx - prev_y(hx)),
            )
            keep_e, gain_e, keep_j, gain_j = (
                coef_ref[i, plane] if final else jnp.concatenate([coef_ref[i, plane], coef[i, plane]], 0) for i in range(4)
            )
            for comp, (old, curl) in enumerate(zip((ex, ey, ez), curls, strict=True)):
                drude = keep_j * field[6 + comp, plane, :keep_rows] + gain_j * old[:keep_rows]
                if not final:
                    field[6 + comp, plane] = drude
                field[comp, plane, :keep_rows] = keep_e * old[:keep_rows] + gain_e * (curl[:keep_rows] - drude)
        if not final:
            side[3], side[4], side[5] = ghx, ghy, ghz
            hy_x, hz_x = turn(ghy, 2 * depth), turn(ghz, 2 * depth)
            curls = (
                (ghz - prev_y(ghz)) - (ghy - hy_above),
                (ghx - hx_above) - (ghz - hz_x),
                (ghy - hy_x) - (ghx - prev_y(ghx)),
            )
            keep_e, gain_e, keep_j, gain_j = (side_coef[i] for i in range(4))
            for comp, (old, curl) in enumerate(zip((gex, gey, gez), curls, strict=True)):
                drude = keep_j * side[6 + comp] + gain_j * old
                side[6 + comp] = drude
                side[comp] = keep_e * old + gain_e * (curl - drude)
        g = table_ref[4 * materials + t - 1]
        g = jnp.concatenate([g] * (rows // 8), 0)
        for plane in range(planes):
            e = [field[i, planes + plane, :rows] for i in range(3)]
            h = [field[3 + i, planes + plane, :rows] for i in range(3)]
            prod = {p: e[p[0]] * e[p[1]] + h[p[0]] * h[p[1]] for p in PAIRS}
            total = {p: g * prod[p] for p in PAIRS}
            if t > 1:
                total = {p: tensor[i, pl.ds(plane * rows, rows), :] + total[p] for i, p in enumerate(PAIRS)}
            if final:
                energy = 0.5 * (total[0, 0] + total[1, 1] + total[2, 2])
                total = {p: v - energy if p[0] == p[1] else v for p, v in total.items()}
            for i, p in enumerate(PAIRS):
                tensor[i, pl.ds(plane * rows, rows), :] = total[p]
        if final:
            own = pl.ds(planes, planes)
            outs = [
                pltpu.make_async_copy(field.at[pl.ds(3 * i, 3), own, pl.ds(0, rows)], out, sems.at[i])
                for i, out in enumerate((e_out, h_out))
            ]
            for copy in outs:
                copy.start()

    def halves(v):
        high = v.astype(jnp.bfloat16)
        return high, (v - high.astype(jnp.float32)).astype(jnp.bfloat16)

    cells = planes * rows
    high, low = halves(tensor[...].reshape(len(PAIRS) * cells, lanes))
    lhs = jnp.concatenate([high, low], 1)
    slots = hot_ref.shape[1]
    owners = n_part * part_outs[0].shape[0]
    chunk = slots
    total = jnp.zeros((2 * owners * 8, TILE_DEV), jnp.float32)
    for at in range(0, slots, chunk):
        here = slice(at, at + chunk)
        in_row, owner, axis = ints_ref[0:1, here], ints_ref[1:2, here], ints_ref[2:3, here]
        hot = hot_ref[:, here]
        picked = jnp.dot(lhs, jnp.concatenate([hot, hot], 0), preferred_element_type=jnp.float32)
        in_row = lax.broadcasted_iota(jnp.int32, (cells, chunk), 0) == in_row
        vals = {
            p: jnp.sum(jnp.where(in_row, picked[i * cells : (i + 1) * cells], 0.0), axis=0, keepdims=True)
            for i, p in enumerate(PAIRS)
        }
        row_force = []
        for i in range(3):
            by = [vals[min(i, a), max(i, a)] for a in range(3)]
            row_force.append(scale_ref[:, here] * jnp.where(axis == 0, by[0], jnp.where(axis == 1, by[1], by[2])))
        stacked = jnp.concatenate(row_force + [jnp.zeros((5, chunk), jnp.float32)], 0)
        spread = jnp.concatenate([jnp.where(owner == o, stacked, 0.0) for o in range(owners)], 0)
        a_high, a_low = halves(spread)
        a = jnp.concatenate([a_high, a_low], 0)
        total = total + lax.dot_general(a, tile_hot_ref[:, here], (((1,), (1,)), ((), ())), preferred_element_type=jnp.float32)
    part = total[: owners * 8] + total[owners * 8 :]
    for o in range(owners):
        part_outs[o % n_part][o // n_part] = part[o * 8 : (o + 1) * 8]
    for copy in outs:
        copy.wait()


def local(sizes, *args):
    return body(sizes, *args)


def body(sizes, e_field, h_field, current, material, sigma_table, gamma_table, plasma_table, g_kernel,
          surf_cell, surf_owner, surf_tile, surf_normal, row_count):
    n_x, n_y, n_z = sizes
    steps = g_kernel.shape[0]
    planes, rows, lanes = material.shape
    f32 = jnp.float32
    _, head, n_msg = slot_order(planes)
    n_pay = n_msg - head
    per_tile = lanes // (2 * steps * planes)
    z_tiles = -(-10 // per_tile)
    n_ghost = 1 if n_y == 2 else 2
    slots = surf_cell.size
    materials = sigma_table.shape[0]
    paired = n_y == 2 and n_x in (2, 4)
    hbm = pl.BlockSpec(memory_space=pltpu.HBM)

    def shape(*dims, dtype=f32):
        return jax.ShapeDtypeStruct(dims, dtype)

    def grant(mib):
        return pltpu.CompilerParams(vmem_limit_bytes=mib << 20)

    def send(value, axis, second=False):
        return lax.ppermute(value, AXES, full_swap(sizes, axis, second))

    small = [
        sigma_table.reshape(1, materials),
        gamma_table.reshape(1, materials),
        plasma_table.reshape(1, materials),
        g_kernel.reshape(1, steps),
    ] + [v.reshape(1, slots) for v in (surf_cell, surf_owner, surf_tile, surf_normal)]
    small = [pltpu.with_memory_space_constraint(v, pltpu.HBM) for v in small]
    args = [v.reshape(3 * planes, rows, lanes) for v in (e_field, h_field, current)] + [material]
    packed = pl.pallas_call(
        functools.partial(pack_kernel, steps, n_ghost),
        out_shape=[shape(n_msg, rows, lanes), shape(n_pay, rows, lanes), shape(n_pay, rows, lanes), shape(z_tiles, rows, lanes)]
        + [shape(z_tiles, 8, lanes)] * n_ghost,
        in_specs=[hbm] * len(args),
        out_specs=[VMEM] * (4 + n_ghost),
        scratch_shapes=[pltpu.VMEM(v.shape, v.dtype) for v in args] + [pltpu.SemaphoreType.DMA((len(args),))],
        compiler_params=grant(4),
        name="pack",
    )(*(pltpu.with_memory_space_constraint(v, pltpu.HBM) for v in args))
    brick, pay_first, pay_second, edge = packed[:4]
    outgoing = packed[4:]

    x_first, x_second = send(pay_first, "gx"), send(pay_second, "gx", True)
    ghosts = [send(v, "gy", bool(i)) for i, v in enumerate(outgoing)]
    edge = pl.pallas_call(
        functools.partial(widen_kernel, steps, n_y),
        out_shape=shape(z_tiles, rows + 8, lanes),
        in_specs=[VMEM] * (1 + n_ghost),
        out_specs=VMEM,
        compiler_params=grant(2),
        name="widen",
    )(edge, *ghosts)
    edges, live_count = pl.pallas_call(
        functools.partial(merge_kernel, steps, n_z),
        out_shape=[shape(z_tiles, rows + 8, lanes), shape(1, lanes, dtype=jnp.int32)],
        in_specs=[SMEM] + [VMEM] * 2,
        out_specs=[VMEM] * 2,
        compiler_params=grant(2),
        name="merge",
    )(row_count, send(edge, "gz"), send(edge, "gz", True))
    edges = [edges, send(edges, "gx"), send(edges, "gx", True)]

    prepare = pl.pallas_call(
        functools.partial(prepare_kernel, n_x, n_y, paired, materials, steps, lanes),
        out_shape=[
            shape(4 * materials + steps, 8, lanes),
            shape(lanes, slots, dtype=jnp.bfloat16),
            shape(TILE_DEV, slots, dtype=jnp.bfloat16),
            shape(8, slots, dtype=jnp.int32),
            shape(1, slots),
            shape(9, 2 * planes, rows, lanes),
            shape(4, 3 * planes, rows, lanes),
        ],
        in_specs=[hbm] * len(small) + [VMEM] * 4,
        out_specs=[VMEM] * 7,
        scratch_shapes=[pltpu.VMEM(v.shape, v.dtype) for v in small] + [pltpu.SemaphoreType.DMA((len(small),))],
        compiler_params=grant(8),
        cost_estimate=pl.CostEstimate(flops=1 << 20, bytes_accessed=1 << 20, transcendentals=0),
        name="prepare",
    )
    bricks = [brick, x_first, x_second]
    prepared = prepare(*small, live_count, *bricks)
    outgoing = pl.pallas_call(
        functools.partial(rows_kernel, steps, len(bricks)),
        out_shape=[shape(-(-(n_msg + 2 * n_pay) // 2), 8, lanes)] * n_ghost,
        in_specs=[VMEM] * len(bricks),
        out_specs=[VMEM] * n_ghost,
        compiler_params=grant(6),
        name="rows",
    )(*bricks)
    ghosts = [send(v, "gy", bool(i)) for i, v in enumerate(outgoing)]

    owners = n_x * n_y
    n_part = n_y if paired else 1
    full = rows + 8
    e_out, h_out, *part = pl.pallas_call(
        functools.partial(main_kernel, sizes, steps, materials, n_ghost, n_part),
        out_shape=[shape(*e_field.shape), shape(*h_field.shape)] + [shape(owners // n_part, 8, TILE_DEV)] * n_part,
        in_specs=[VMEM] * (len(bricks) + n_ghost + len(edges) + len(prepared)),
        out_specs=[hbm, hbm] + [VMEM] * n_part,
        scratch_shapes=[
            pltpu.VMEM((10, 3 * planes, full, lanes), f32),
            pltpu.VMEM((4, 3 * planes, full - rows, lanes), f32),
            pltpu.VMEM((10, full, lanes), f32),
            pltpu.VMEM((4, full, lanes), f32),
            pltpu.VMEM((len(PAIRS), planes * rows, lanes), f32),
            pltpu.SemaphoreType.DMA((2,)),
        ],
        compiler_params=grant(24),
        name="march",
    )(*bricks, *ghosts, *edges, *prepared)
    if not paired:
        got = lax.all_to_all(part[0], ("gx", "gy"), split_axis=0, concat_axis=0, tiled=True)
        return e_out, h_out, jnp.sum(got[:, :3], axis=0)
    near = part[0] + send(part[1], "gy")
    near = near[:, :4]
    force = near[0]
    for d in range(n_x - 1, 0, -1):
        pairs = [
            ((a * n_y + b) * n_z + c, ((a ^ d) * n_y + b) * n_z + c) for a in range(n_x) for b in range(n_y) for c in range(n_z)
        ]
        force = force + lax.ppermute(near[d], AXES, pairs)
    return e_out, h_out, force[:3]


def solution(mesh):
    sizes = tuple(mesh.shape[a] for a in AXES)
    return jax.shard_map(
        functools.partial(local, sizes),
        mesh=mesh,
        in_specs=(
            P(None, "gx", "gy", "gz"),
            P(None, "gx", "gy", "gz"),
            P(None, "gx", "gy", "gz"),
            P("gx", "gy", "gz"),
            P(),
            P(),
            P(),
            P(),
            P("gx", "gy", "gz", None),
            P("gx", "gy", "gz", None, None),
            P("gx", "gy", "gz", None),
            P("gx", "gy", "gz", None),
            P("gx", "gy", "gz"),
        ),
        out_specs=(
            P(None, "gx", "gy", "gz"),
            P(None, "gx", "gy", "gz"),
            P(None, ("gx", "gy", "gz")),
        ),
        check_vma=False,
    )
```
